256 devices in a mesh: tm: 8 (over x_lo, y), space: 32 (over z, x_hi, core).
Axes of the slice: x: 4 (x_hi: 2, x_lo: 2; x = x_hi * 2 + x_lo), y: 4, z: 8, core: 2. Of those that a mesh axis runs over, the one named last changes fastest.
Arguments:
- guess: float32 [16, 1024, 4096], P('tm', 'space'), may hold values from -6 to 6
- sources: bfloat16 [64, 1024, 4096], P('tm', 'space'), may hold values from -6 to 6
- velocity: bfloat16 [4, 2, 1024, 4096], P(None, None, 'space'), may hold values from -1 to 1
- snapshot: int32 [64], replicated, may hold values from 0 to 3
Outputs:
- c_values: float32 [16, 1024, 4096], P('tm', 'space')
- control_grad: float32 [1024, 4096], P('space', 'tm')
The draws below stay inside these ranges and needn't reach their ends.
Inputs may be any that keep to these rules, and one draw needn't show every extreme that they name: Each entry names a stored snapshot.
All inputs are finite; a program needn't handle non-finite values.
Results may differ from the reference program's by a relative error of at most 0.0003.
Values may be sent and summed in bfloat16 or wider, within the bound.
No kernel may reach another device: no remote copies, remote signals or barrier semaphores. Data moves between devices by JAX's collectives and lax.ppermute only.
A program may use at most 128 MiB of HBM per device.

```python
import jax
import jax.numpy as jnp
from jax import lax

COLS = 4096
CF = 4
NSNAP = 4
NT = 64
NC = 16
NX = 1024


def with_ends(values, key, low, top_value):
    longest = values.shape.index(max(values.shape))
    spots = []
    for shift in (0, 1):
        where = [jax.random.randint(jax.random.fold_in(key, axis), (), 0, length) for axis, length in enumerate(values.shape)]
        where[longest] = (where[longest] + shift) % values.shape[longest]
        spots.append(tuple(where))
    return values.at[spots[0]].set(low).at[spots[1]].set(top_value)


def levels(stream_key, dims, shards, least, top_value):
    factor_of, own = 1.0, jax.random.fold_in(stream_key, 6)
    for position, shards_of in shards:
        steps = jnp.exp(jax.random.uniform(jax.random.fold_in(own, position), (shards_of,), jnp.float32, least / len(shards), top_value / len(shards)))
        factor_of = factor_of * jnp.repeat(steps, dims[position] // shards_of).reshape([-1 if axis == position else 1 for axis in range(len(dims))])
    return factor_of


def noise(own_key, shape, width, most, split=(), kind=jnp.bfloat16):
    factor_of = levels(own_key, shape, split, -0.22, 0.18) if split else 1.0
    result = jax.random.normal(own_key, shape, jnp.float32) * width * factor_of
    return jnp.minimum(jnp.maximum(result, -most), most).astype(kind)


def setup_inputs(seed: int = 0) -> dict:
    key_list = jax.random.split(jax.random.key(seed), 5)
    guess = noise(key_list[0], (NC, NX, COLS), 1.0, 6.0, ((0, 8), (1, 32)), jnp.float32)
    sources = noise(key_list[1], (NT, NX, COLS), 1.0, 6.0, ((0, 8), (1, 32)))
    velocity = jnp.clip(jax.random.uniform(key_list[2], (NSNAP, 2, NX, COLS), jnp.float32, -1.0, 1.0) * levels(key_list[2], (NSNAP, 2, NX, COLS), ((2, 32),), -0.4, 0.0), -1.0, 1.0).astype(jnp.bfloat16)
    snapshot = with_ends(jax.random.randint(key_list[3], (NT,), 0, NSNAP), jax.random.fold_in(key_list[3], 1), 0, NSNAP - 1).astype(jnp.int32)
    return dict(guess=guess, sources=sources, velocity=velocity, snapshot=snapshot)


FINE_DIFF = 0.2
FINE_ADV = 0.3
COARSE_DIFF = 0.24
COARSE_ADV = 0.4


def shift_east(field):
    return jnp.concatenate([field[..., 1:], jnp.zeros_like(field[..., :1])], -1)


def shift_west(field):
    return jnp.concatenate([jnp.zeros_like(field[..., :1]), field[..., :-1]], -1)


def adjoint_step(state, speeds, diff, adv):
    speed_x = speeds[..., 0, :, :].astype(jnp.float32)
    speed_y = speeds[..., 1, :, :].astype(jnp.float32)
    centre = state[..., 1:-1, :]
    flux_x = speed_x * state
    flux_y = (speed_y * state)[..., 1:-1, :]
    laplace = state[..., 2:, :] + state[..., :-2, :] + shift_east(centre) + shift_west(centre) - 4.0 * centre
    advected = flux_x[..., 2:, :] - flux_x[..., :-2, :] + shift_east(flux_y) - shift_west(flux_y)
    return centre + diff * laplace + 0.5 * adv * advected


def pad_rows(field):
    widths = [(0, 0)] * (field.ndim - 2) + [(1, 1), (0, 0)]
    return jnp.pad(field, widths)


def reference(guess, sources, velocity, snapshot):
    def full_step(state, moment, diff, adv):
        speeds = lax.dynamic_index_in_dim(velocity, snapshot[moment], 0, keepdims=False)
        return adjoint_step(pad_rows(state), pad_rows(speeds), diff, adv)

    def relax(coarse_vals):
        tops = jnp.concatenate([coarse_vals[1:], jnp.zeros_like(coarse_vals[:1])], 0)

        def one_interval(items):
            state, interval = items
            time_total = jnp.zeros_like(state)
            for offset in range(CF - 1, 0, -1):
                moment = interval * CF + offset
                source = lax.dynamic_index_in_dim(sources, moment, 0, keepdims=False)
                state = full_step(state, moment, FINE_DIFF, FINE_ADV) + source.astype(jnp.float32)
                time_total = time_total + state
            return state, time_total

        return lax.map(one_interval, (tops, jnp.arange(NC, dtype=jnp.int32)))

    lowest, _ = relax(guess)

    def residual_of(items):
        state, interval, current = items
        moment = interval * CF
        source = lax.dynamic_index_in_dim(sources, moment, 0, keepdims=False)
        return full_step(state, moment, FINE_DIFF, FINE_ADV) + source.astype(jnp.float32) - current

    residual = lax.map(residual_of, (lowest, jnp.arange(NC, dtype=jnp.int32), guess))

    def coarse_fn(correction, items):
        res_term, interval = items
        correction = full_step(correction, interval * CF, COARSE_DIFF, COARSE_ADV) + res_term
        return correction, correction

    _, corr = lax.scan(coarse_fn, jnp.zeros_like(guess[0]), (residual, jnp.arange(NC, dtype=jnp.int32)), reverse=True)
    c_values = guess + corr
    _, f_totals = relax(c_values)
    control_grad = (jnp.sum(c_values, 0) + jnp.sum(f_totals, 0)) / NT
    return c_values, control_grad
```

```python
import functools

import jax
import jax.numpy as jnp
from jax import lax
from jax.experimental import pallas as pl
from jax.experimental.pallas import tpu as pltpu
from jax.sharding import PartitionSpec as P

FINE_DIFF = 0.2
FINE_ADV = 0.3
COARSE_DIFF = 0.24
COARSE_ADV = 0.4

F32 = jnp.float32
LINK = jnp.float16
LANE = 128
SUB = 8
ROWS = 32
COLS = 4096
CHUNK = 512
WIDE = 640
PAD = COLS + 2 * LANE
NEAR = 40
FAR = 72
NDEV = 8
NCOARSE = 16
TILES = COLS // LANE
LIMIT = 62 * 1024 * 1024

VM = pl.BlockSpec(memory_space=pltpu.VMEM)
SM = pl.BlockSpec(memory_space=pltpu.SMEM)


def halo_tiles():
    return [(j, 1 if j <= 6 else (2 if j < 15 else 3)) for j in range(1, NCOARSE)]


def call(kernel, outs, args, scratch=(), flops=10_000_000):
    specs = [SM if a.dtype == jnp.int32 else VM for a in args]
    nbytes = sum(a.size * a.dtype.itemsize for a in args)
    return pl.pallas_call(
        kernel,
        out_shape=outs,
        in_specs=specs,
        out_specs=jax.tree.map(lambda _: VM, outs),
        scratch_shapes=list(scratch),
        compiler_params=pltpu.CompilerParams(vmem_limit_bytes=LIMIT),
        cost_estimate=pl.CostEstimate(flops=flops, bytes_accessed=nbytes, transcendentals=0),
    )(*args)


def sub_iota(cols):
    return lax.broadcasted_iota(jnp.int32, (SUB, cols), 0)


def lane_iota(rows):
    return lax.broadcasted_iota(jnp.int32, (rows, LANE), 1)


def roll4(x):
    return pltpu.roll(x, 4, 0)


def up(x):
    return pltpu.roll(x, x.shape[0] - 1, 0)


def down(x):
    return pltpu.roll(x, 1, 0)


def east(x):
    return pltpu.roll(x, x.shape[1] - 1, 1)


def west(x):
    return pltpu.roll(x, 1, 1)


def pack_inputs(guess, sources, velocity, out_a, out_b):
    t = lax.axis_index("tm")
    odd = lax.rem(lax.axis_index("space"), 2) == 1
    low = sub_iota(COLS) < 4

    def put(n, top, bottom):
        out_a[n * SUB : (n + 1) * SUB, :] = jnp.where(odd, top, bottom).astype(jnp.bfloat16)
        out_b[n * SUB : (n + 1) * SUB, :] = jnp.where(odd, bottom, top).astype(jnp.bfloat16)

    def pair(n, read_x, read_y):
        x0, y0 = read_x(0), read_y(0)
        x3, y3 = read_x(24), read_y(24)
        put(n, jnp.where(low, x0, roll4(y0)), jnp.where(low, roll4(x3), y3))

    def rows(ref, *at):
        return lambda r: ref[(*at, pl.ds(r, SUB), slice(None))].astype(F32)

    for k in range(4):
        pair(k, rows(velocity, k, 0), rows(velocity, k, 1))
    for i, n in enumerate((3, 2, 1)):
        pair(4 + i, rows(sources, n), rows(sources, n + 4))
    pair(7, rows(guess, 1), rows(guess, 0))

    base = pl.multiple_of(t * CHUNK, LANE)
    left = pl.multiple_of(jnp.maximum(t * CHUNK - LANE, 0), LANE)
    right = pl.multiple_of(jnp.minimum(t * CHUNK + CHUNK, COLS - LANE), LANE)
    half = lane_iota(SUB) < 64
    sub = sub_iota(LANE)

    def wide(k, c, r, l):
        if l < 4:
            return velocity[k, c, pl.ds(r, SUB), pl.ds(base + l * LANE, LANE)].astype(F32)
        a = velocity[k, c, pl.ds(r, SUB), pl.ds(right, LANE)].astype(F32)
        b = velocity[k, c, pl.ds(r, SUB), pl.ds(left, LANE)].astype(F32)
        return jnp.where(half, a, b)

    def place(q, top, bottom):
        r, l = 8 + q // TILES, q % TILES
        at = (slice(r * SUB, (r + 1) * SUB), slice(l * LANE, (l + 1) * LANE))
        out_a[at] = jnp.where(odd, top, bottom).astype(jnp.bfloat16)
        out_b[at] = jnp.where(odd, bottom, top).astype(jnp.bfloat16)

    for k in range(4):
        for c in range(2):
            for l in range(5):
                for half_no in range(2):
                    q = ((k * 2 + c) * 2 + half_no) * 5 + l
                    place(q, wide(k, c, 8 * half_no, l), wide(k, c, 24 - 8 * half_no, l))
    for l in range(5):
        top = jnp.zeros((SUB, LANE), F32)
        bottom = top
        for k in range(4):
            a, b = wide(k, 0, 16, l), wide(k, 0, 8, l)
            top = jnp.where(sub == k, pltpu.roll(a, k, 0) if k else a, top)
            bottom = jnp.where(sub == k, pltpu.roll(b, k + 1, 0), bottom)
        place(80 + l, top, bottom)
    for q in range(85, 3 * TILES):
        place(q, jnp.zeros((SUB, LANE), F32), jnp.zeros((SUB, LANE), F32))


def swap(buf_a, buf_b):
    count = lax.axis_size("space")
    pairs_b = [(i, i + 1) for i in range(1, count - 1, 2)]
    pairs_b = pairs_b + [(j, i) for i, j in pairs_b]
    pairs_a = [(i, i ^ 1) for i in range(count)]
    got_b = lax.ppermute(buf_b, "space", pairs_b)
    got_a = lax.ppermute(buf_a, "space", pairs_a)
    return got_a, got_b


def fine_ext(p, l0, vel, snap, width):
    mid = pl.multiple_of(l0 + LANE, LANE)
    pe = p[:, pl.ds(mid, width + LANE)]
    pw = p[:, pl.ds(pl.multiple_of(l0, LANE), width + LANE)]
    pc = p[:, pl.ds(mid, width)]
    ax = vel[snap, 0, :, pl.ds(mid, width)]
    ye = vel[snap, 1, :, pl.ds(mid, width + LANE)]
    yw = vel[snap, 1, :, pl.ds(pl.multiple_of(l0, LANE), width + LANE)]
    u = FINE_DIFF * pc
    wx = ax * pc
    out = (1.0 - 4.0 * FINE_DIFF) * pc + up(u + wx) + down(u - wx)
    ge = (FINE_DIFF + ye) * pe
    gw = (FINE_DIFF - yw) * pw
    return out + east(ge)[:, :width] + west(gw)[:, LANE:]


def first_relax(snapshot, guess, sources, velocity, got_a, got_b, pay, base, vel, s_halo, pa, pb, acc, res):
    t = lax.axis_index("tm")
    s = lax.axis_index("space")
    odd = lax.rem(s, 2) == 1
    first = t * 8
    low = sub_iota(COLS) < 4
    has_above = (s > 0).astype(F32)
    has_below = (s < lax.axis_size("space") - 1).astype(F32)
    inner = (t > 0).astype(F32)

    def halves(n):
        a = got_a[n * SUB : (n + 1) * SUB, :].astype(F32)
        b = got_b[n * SUB : (n + 1) * SUB, :].astype(F32)
        below, above = jnp.where(odd, b, a), jnp.where(odd, a, b)
        return jnp.where(low, below, roll4(above)), jnp.where(low, roll4(below), above)

    zero = jnp.zeros((NEAR, LANE), F32)
    for buf in (pa, pb):
        buf[:, :LANE] = zero
        buf[:, PAD - LANE :] = zero
    for n in range(4):
        res[n, :, :LANE] = zero[:ROWS]
        res[n, :, PAD - LANE :] = zero[:ROWS]
    mid = slice(LANE, PAD - LANE)
    for k in range(4):
        hx, hy = halves(k)
        for c, h in ((0, hx), (1, hy)):
            vel[k, c, :, :LANE] = zero
            vel[k, c, :, PAD - LANE :] = zero
            vel[k, c, :ROWS, mid] = (0.5 * FINE_ADV) * velocity[k, c].astype(F32)
            vel[k, c, ROWS:, mid] = (0.5 * FINE_ADV) * h
    for i, n in enumerate((3, 2, 1)):
        hx, hy = halves(4 + i)
        s_halo[n] = hx
        s_halo[n + 4] = hy
    g1, g0 = halves(7)

    width = CHUNK
    sub = sub_iota(width)
    edge = jnp.where(sub < 4, has_below, has_above)

    def step(src, dst, snap, source, accumulate):
        def go(i, carry):
            l0 = i * width
            out = fine_ext(src, l0, vel, snap, width)
            at = pl.ds(pl.multiple_of(l0, LANE), width)
            own, far = out[:ROWS], out[ROWS:] * edge
            if source is not None:
                own = own + sources[source, :, at].astype(F32)
                far = far + s_halo[source, :, at]
            to = pl.ds(pl.multiple_of(l0 + LANE, LANE), width)
            dst[:ROWS, to] = own
            dst[ROWS:, to] = far
            acc[:, at] = acc[:, at] + own
            return carry

        lax.fori_loop(0, COLS // width, go, 0)

    def last(src, snap, source, n, level):
        def go(i, carry):
            l0 = i * width
            own = fine_ext(src, l0, vel, snap, width)[:ROWS]
            at = pl.ds(pl.multiple_of(l0, LANE), width)
            to = pl.ds(pl.multiple_of(l0 + LANE, LANE), width)
            if source is not None:
                own = own + sources[source, :, at].astype(F32)
                base[level, :, at] = own
                own = own - guess[level, :, at]
            res[n, :, to] = own
            return carry

        lax.fori_loop(0, COLS // width, go, 0)

    acc[...] = guess[0] + guess[1]
    pa[:ROWS, mid] = guess[1]
    pa[ROWS:, mid] = g1
    step(pa, pb, snapshot[first + 3], 3, True)
    step(pb, pa, snapshot[first + 2], 2, True)
    step(pa, pb, snapshot[first + 1], 1, True)
    last(pb, snapshot[first], 0, 0, 0)
    pa[:ROWS, mid] = sources[7].astype(F32)
    pa[ROWS:, mid] = s_halo[7]
    acc[...] = acc[...] + sources[7].astype(F32)
    step(pa, pb, snapshot[first + 6], 6, True)
    step(pb, pa, snapshot[first + 5], 5, True)
    last(pa, snapshot[first + 4], 4, 1, 1)
    pa[:ROWS, mid] = guess[0] * inner
    pa[ROWS:, mid] = g0 * inner
    before = jnp.maximum(first - 4, 0)
    step(pa, pb, snapshot[before + 3], None, True)
    step(pb, pa, snapshot[before + 2], None, True)
    step(pa, pb, snapshot[before + 1], None, True)
    last(pb, snapshot[before], None, 2, None)
    res[3, :, mid] = acc[...]

    half = lane_iota(ROWS) < 64
    for n in range(4):
        for d in range(NDEV):
            at = LANE + d * CHUNK
            pay[d, n, :, :CHUNK] = res[n, :, at : at + CHUNK]
            right = res[n, :, at + CHUNK : at + CHUNK + LANE]
            left = res[n, :, at - LANE : at]
            pay[d, n, :, CHUNK:] = jnp.where(half, right, left)


def level_rows(got, j, r):
    t, u = divmod(j, 2)
    value = got[t, u, r : r + SUB, :]
    if u == 1 and t + 1 < NDEV:
        value = value + got[t + 1, 2, r : r + SUB, :]
    return value


def pack_residual(got, out_a, out_b):
    odd = lax.rem(lax.axis_index("space"), 2) == 1
    n = 0
    for j, count in halo_tiles():
        for i in range(count):
            top, bottom = level_rows(got, j, 8 * i), level_rows(got, j, 24 - 8 * i)
            out_a[n * SUB : (n + 1) * SUB, :] = jnp.where(odd, top, bottom)
            out_b[n * SUB : (n + 1) * SUB, :] = jnp.where(odd, bottom, top)
            n += 1


def coarse_solve(snapshot, got, velocity, in_a, in_b, got_a, got_b, back, near, vnear, part, vel, res, mask):
    t = lax.axis_index("tm")
    s = lax.axis_index("space")
    odd = lax.rem(s, 2) == 1
    has_above = (s > 0).astype(F32)
    has_below = (s < lax.axis_size("space") - 1).astype(F32)
    has_left = (t > 0).astype(F32)
    has_right = (t < lax.axis_size("tm") - 1).astype(F32)
    row = lax.broadcasted_iota(jnp.int32, (FAR, WIDE), 0)
    col = lax.broadcasted_iota(jnp.int32, (FAR, WIDE), 1)
    in_rows = jnp.where(row < ROWS, 1.0, jnp.where(row < 52, has_below, has_above))
    in_cols = jnp.where(col < CHUNK, 1.0, jnp.where(col < CHUNK + 64, has_right, has_left))
    mask[...] = in_rows * in_cols

    base = pl.multiple_of(t * CHUNK, LANE)
    left = pl.multiple_of(jnp.maximum(t * CHUNK - LANE, 0), LANE)
    right = pl.multiple_of(jnp.minimum(t * CHUNK + CHUNK, COLS - LANE), LANE)
    half = lane_iota(ROWS) < 64
    sub = sub_iota(LANE)
    low = sub < 4

    def tile(q):
        r, l = 8 + q // TILES, q % TILES
        at = (slice(r * SUB, (r + 1) * SUB), slice(l * LANE, (l + 1) * LANE))
        a, b = in_a[at].astype(F32), in_b[at].astype(F32)
        return jnp.where(odd, b, a), jnp.where(odd, a, b)

    fine = 0.5 * FINE_ADV
    coarse = 0.5 * COARSE_ADV
    for k in range(4):
        for c in range(2):
            for l in range(5):
                lanes = slice(l * LANE, (l + 1) * LANE)
                if l < 4:
                    own = velocity[k, c, :, pl.ds(base + l * LANE, LANE)].astype(F32)
                else:
                    own = jnp.where(
                        half,
                        velocity[k, c, :, pl.ds(right, LANE)].astype(F32),
                        velocity[k, c, :, pl.ds(left, LANE)].astype(F32),
                    )
                q = (k * 2 + c) * 10 + l
                below0, above0 = tile(q)
                below1, above1 = tile(q + 5)
                edge = jnp.zeros((SUB, LANE), F32)
                if c == 0:
                    below, above = tile(80 + l)
                    shifted = pltpu.roll(below, SUB - k, 0) if k else below
                    edge = jnp.where(sub == 0, shifted, edge)
                    edge = jnp.where(sub == 7, pltpu.roll(above, 7 - k, 0), edge)
                vel[k, c, :ROWS, lanes] = coarse * own
                vel[k, c, 32:40, lanes] = coarse * below0
                vel[k, c, 40:48, lanes] = coarse * below1
                vel[k, c, 48:56, lanes] = coarse * edge
                vel[k, c, 56:64, lanes] = coarse * above1
                vel[k, c, 64:72, lanes] = coarse * above0
                vnear[k, c, :ROWS, lanes] = fine * own
                vnear[k, c, ROWS:, lanes] = fine * jnp.where(low, below0, above0)

    n = 0
    low_w = sub_iota(WIDE) < 4
    empty = jnp.zeros((SUB, WIDE), F32)
    for j, count in halo_tiles():
        tiles = []
        for i in range(count):
            a, b = got_a[n * SUB : (n + 1) * SUB, :], got_b[n * SUB : (n + 1) * SUB, :]
            tiles.append((jnp.where(odd, b, a), jnp.where(odd, a, b)))
            n += 1
        res[j, 32:40, :] = tiles[0][0]
        res[j, 64:72, :] = tiles[0][1]
        res[j, 40:48, :] = tiles[1][0] if count > 1 else empty
        res[j, 56:64, :] = tiles[1][1] if count > 1 else empty
        res[j, 48:56, :] = jnp.where(low_w, *tiles[2]) if count > 2 else empty
    res[0, ROWS:, :] = jnp.zeros((FAR - ROWS, WIDE), F32)
    for j in range(NCOARSE):
        res[j, :ROWS, :] = got[j // 2, j % 2]

    total = got[0, 3, :, :CHUNK]
    for d in range(1, NDEV):
        total = total + got[d, 3, :, :CHUNK]
    part[...] = total

    def send(j, p, e):
        back[j // 2, j % 2] = e[:ROWS, :CHUNK]
        near[j, :ROWS, :] = p[:ROWS]
        near[j, ROWS:, :] = jnp.where(low_w, p[32:40], p[64:72])
        part[...] = part[...] + p[:ROWS, :CHUNK]

    p = res[NCOARSE - 1]
    send(NCOARSE - 1, p, jnp.zeros_like(p))
    for j in range(NCOARSE - 2, -1, -1):
        snap = snapshot[4 * j]
        ax, ay = vel[snap, 0], vel[snap, 1]
        u = COARSE_DIFF * p
        wx = ax * p
        wy = ay * p
        e = (1.0 - 4.0 * COARSE_DIFF) * p + up(u + wx) + down(u - wx) + east(u + wy) + west(u - wy)
        e = e * mask[...]
        if j % 2 == 1:
            head = e[:ROWS] + got[j // 2 + 1, 2]
            e = jnp.concatenate([head, e[ROWS:]], 0)
        p = e + res[j]
        send(j, p, e)


def second_relax(snapshot, near, vnear, part, grad, acc):
    t = lax.axis_index("tm")
    s = lax.axis_index("space")
    has_above = (s > 0).astype(F32)
    has_below = (s < lax.axis_size("space") - 1).astype(F32)
    has_left = (t > 0).astype(F32)
    has_right = (t < lax.axis_size("tm") - 1).astype(F32)
    row = lax.broadcasted_iota(jnp.int32, (NEAR, WIDE), 0)
    col = lax.broadcasted_iota(jnp.int32, (NEAR, WIDE), 1)
    in_rows = jnp.where(row < ROWS, 1.0, jnp.where(row < 36, has_below, has_above))
    in_cols = jnp.where(col < CHUNK, 1.0, jnp.where(col < CHUNK + 64, has_right, has_left))
    mask = in_rows * in_cols
    acc[...] = part[...]

    def interval(j, carry):
        p = near[j + 1]
        for k in (3, 2, 1):
            snap = snapshot[4 * j + k]
            ax, ay = vnear[snap, 0], vnear[snap, 1]
            u = FINE_DIFF * p
            wx = ax * p
            wy = ay * p
            e = (1.0 - 4.0 * FINE_DIFF) * p + up(u + wx) + down(u - wx) + east(u + wy) + west(u - wy)
            p = e * mask
            acc[...] = acc[...] + p[:ROWS, :CHUNK]
        return carry

    lax.fori_loop(0, NCOARSE - 1, interval, 0)
    grad[...] = acc[...] * (1.0 / 64.0)


def finish(base, got, out):
    for d in range(NDEV):
        at = slice(d * CHUNK, (d + 1) * CHUNK)
        for u in range(2):
            out[u, :, at] = base[u, :, at] + got[d, u]


def body(guess, sources, velocity, snapshot):
    shape = jax.ShapeDtypeStruct
    bf = jnp.bfloat16
    packed = shape((88, COLS), bf)
    send_a, send_b = call(pack_inputs, (packed, packed), (guess, sources, velocity))
    in_a, in_b = swap(send_a, send_b)
    pay, base = call(
        first_relax,
        (shape((NDEV, 4, ROWS, WIDE), F32), shape((2, ROWS, COLS), F32)),
        (snapshot, guess, sources, velocity, in_a, in_b),
        (
            pltpu.VMEM((4, 2, NEAR, PAD), F32),
            pltpu.VMEM((8, SUB, COLS), F32),
            pltpu.VMEM((NEAR, PAD), F32),
            pltpu.VMEM((NEAR, PAD), F32),
            pltpu.VMEM((ROWS, COLS), F32),
            pltpu.VMEM((4, ROWS, PAD), F32),
        ),
    )
    got = lax.all_to_all(pay.astype(LINK), "tm", 0, 0, tiled=False).astype(F32)
    tiles = sum(count for _, count in halo_tiles())
    edges = shape((tiles * SUB, WIDE), F32)
    send_a, send_b = call(pack_residual, (edges, edges), (got,))
    got_a, got_b = swap(send_a.astype(LINK), send_b.astype(LINK))
    back, near, vnear, part = call(
        coarse_solve,
        (
            shape((NDEV, 2, ROWS, CHUNK), F32),
            shape((NCOARSE, NEAR, WIDE), F32),
            shape((4, 2, NEAR, WIDE), F32),
            shape((ROWS, CHUNK), F32),
        ),
        (snapshot, got, velocity, in_a, in_b, got_a.astype(F32), got_b.astype(F32)),
        (
            pltpu.VMEM((4, 2, FAR, WIDE), F32),
            pltpu.VMEM((NCOARSE, FAR, WIDE), F32),
            pltpu.VMEM((FAR, WIDE), F32),
        ),
    )
    returned = lax.all_to_all(back.astype(LINK), "tm", 0, 0, tiled=False)
    grad = call(
        second_relax,
        shape((ROWS, CHUNK), F32),
        (snapshot, near, vnear, part),
        (pltpu.VMEM((ROWS, CHUNK), F32),),
    )
    c_values = call(finish, shape((2, ROWS, COLS), F32), (base, returned.astype(F32)))
    return c_values, grad


def solution(mesh):
    in_specs = (P("tm", "space", None), P("tm", "space", None), P(None, None, "space", None), P())
    out_specs = (P("tm", "space", None), P("space", "tm"))
    return jax.shard_map(body, mesh=mesh, in_specs=in_specs, out_specs=out_specs, check_vma=False)
```

```python
import jax
import jax.numpy as jnp
from jax import lax
from jax.experimental import pallas as pl
from jax.experimental.pallas import tpu as pltpu
from jax.sharding import PartitionSpec as P


FINE_DIFF = 0.2
FINE_ADV = 0.3
COARSE_DIFF = 0.24
COARSE_ADV = 0.4

F32 = jnp.float32
LINK = jnp.float16
LANE = 128
SUB = 8
ROWS = 32
COLS = 4096
CHUNK = 512
WIDE = 640
PAD = COLS + 2 * LANE
NEAR = 40
FAR = 72
NDEV = 8
NCOARSE = 16
GROUP = 3
MIB = 1024 * 1024

VM = pl.BlockSpec(memory_space=pltpu.VMEM)
SM = pl.BlockSpec(memory_space=pltpu.SMEM)


def halo_tiles():
    return [(j, 1 if j <= 6 else (2 if j < 15 else 3)) for j in range(1, NCOARSE)]


def call(kernel, outs, args, scratch=(), flops=10_000_000, vmem=16, space=pltpu.VMEM):
    specs = [SM if a.dtype == jnp.int32 else pl.BlockSpec(memory_space=space) for a in args]
    nbytes = sum(a.size * a.dtype.itemsize for a in args)
    return pl.pallas_call(
        kernel,
        out_shape=outs,
        in_specs=specs,
        out_specs=jax.tree.map(lambda _: VM, outs),
        scratch_shapes=list(scratch),
        compiler_params=pltpu.CompilerParams(vmem_limit_bytes=vmem * MIB),
        cost_estimate=pl.CostEstimate(flops=flops, bytes_accessed=nbytes, transcendentals=0),
    )(*args)


def sub_iota(cols):
    return lax.broadcasted_iota(jnp.int32, (SUB, cols), 0)


def lane_iota(rows):
    return lax.broadcasted_iota(jnp.int32, (rows, LANE), 1)


def roll4(x):
    return pltpu.roll(x, 4, 0)


def up(x):
    return pltpu.roll(x, x.shape[0] - 1, 0)


def down(x):
    return pltpu.roll(x, 1, 0)


def east(x):
    return pltpu.roll(x, x.shape[1] - 1, 1)


def west(x):
    return pltpu.roll(x, 1, 1)


def pack_fine(guess, sources, velocity, out_a, out_b, guess_v, sources_v, velocity_v, sems):
    odd = lax.rem(lax.axis_index("space"), 2) == 1
    copies = [pltpu.make_async_copy(velocity.at[k], velocity_v.at[k], sems.at[k]) for k in range(4)]
    copies.append(pltpu.make_async_copy(guess, guess_v, sems.at[4]))
    copies.append(pltpu.make_async_copy(sources, sources_v, sems.at[5]))
    for copy in copies:
        copy.start()
    first, final = slice(0, SUB), slice(ROWS - SUB, ROWS)
    vt, vb = velocity_v.at[:, :, first, :], velocity_v.at[:, :, final, :]
    st, sb = sources_v.at[:, first, :], sources_v.at[:, final, :]
    gt, gb = guess_v.at[:, first, :], guess_v.at[:, final, :]
    sub = sub_iota(COLS)
    low = sub < 4

    def put(n, top, bottom):
        out_a[n * SUB : (n + 1) * SUB, :] = jnp.where(odd, top, bottom).astype(jnp.bfloat16)
        out_b[n * SUB : (n + 1) * SUB, :] = jnp.where(odd, bottom, top).astype(jnp.bfloat16)

    def pair(n, x0, y0, x3, y3):
        put(n, jnp.where(low, x0, roll4(y0)), jnp.where(low, roll4(x3), y3))

    for k in range(4):
        copies[k].wait()
        pair(k, *(ref[k, c].astype(F32) for ref in (vt, vb) for c in (0, 1)))
    copies[4].wait()
    pair(4, gt[1], gt[0], gb[1], gb[0])
    copies[5].wait()
    pair(5, *(ref[n].astype(F32) for ref in (st, sb) for n in (3, 7)))
    top, bottom = st[2].astype(F32), pltpu.roll(sb[2].astype(F32), 2, 0)
    for i, n in enumerate((1, 6, 5)):
        here = sub >= 2 * i + 2
        top = jnp.where(here, pltpu.roll(st[n].astype(F32), 2 * i + 2, 0), top)
        more = sb[n].astype(F32)
        more = pltpu.roll(more, 2 * i + 4, 0) if i < 2 else more
        bottom = jnp.where(here, more, bottom)
    put(6, top, bottom)


FINE_TILES = 7
COARSE_TILES = 17


def chunk_at(t):
    base = pl.multiple_of(t * CHUNK, LANE)
    left = pl.multiple_of(jnp.maximum(t * CHUNK - LANE, 0), LANE)
    right = pl.multiple_of(jnp.minimum(t * CHUNK + CHUNK, COLS - LANE), LANE)
    return base, left, right


def pack_coarse(velocity, out_a, out_b):
    odd = lax.rem(lax.axis_index("space"), 2) == 1
    sub = sub_iota(WIDE)
    wide = lambda k, c, r: velocity[k, c, r : r + SUB, :].astype(F32)

    def place(n, top, bottom):
        at = slice(n * SUB, (n + 1) * SUB)
        out_a[at, :] = jnp.where(odd, top, bottom).astype(jnp.bfloat16)
        out_b[at, :] = jnp.where(odd, bottom, top).astype(jnp.bfloat16)

    for k in range(4):
        for c in range(2):
            for i in range(2):
                place((k * 2 + c) * 2 + i, wide(k, c, 8 * i), wide(k, c, 24 - 8 * i))
    top = jnp.zeros((SUB, WIDE), F32)
    bottom = top
    for k in range(4):
        x, y = wide(k, 0, 16), wide(k, 0, 8)
        top = jnp.where(sub == k, pltpu.roll(x, k, 0) if k else x, top)
        bottom = jnp.where(sub == k, pltpu.roll(y, k + 1, 0), bottom)
    place(16, top, bottom)


def swap(buf_a, buf_b):
    count = lax.axis_size("space")
    pairs_b = [(i, i + 1) for i in range(1, count - 1, 2)]
    pairs_b = pairs_b + [(j, i) for i, j in pairs_b]
    pairs_a = [(i, i ^ 1) for i in range(count)]
    got_b = lax.ppermute(buf_b, "space", pairs_b)
    got_a = lax.ppermute(buf_a, "space", pairs_a)
    return got_a, got_b


MID = slice(LANE, PAD - LANE)


def fine_step(p, coef, l0, width):
    at = pl.multiple_of(l0, LANE)
    mid = pl.multiple_of(l0 + LANE, LANE)
    pc = p[:, pl.ds(mid, width)]
    out = (1.0 - 4.0 * FINE_DIFF) * pc
    out = out + up(coef(0, mid, width) * pc) + down(coef(1, mid, width) * pc)
    ge = coef(2, mid, width + LANE) * p[:, pl.ds(mid, width + LANE)]
    gw = coef(3, at, width + LANE) * p[:, pl.ds(at, width + LANE)]
    return out + east(ge)[:, :width] + west(gw)[:, LANE:]


def coefficients(c, v):
    half = 0.5 * FINE_ADV * v
    return ((2 * c, FINE_DIFF + half), (2 * c + 1, FINE_DIFF - half))


def relax_chains(t, snapshot, step, last, start, pa, pb):
    first = t * 8
    start(pa, "second")
    step(pa, pb, snapshot[first + 3], 3)
    step(pb, pa, snapshot[first + 2], 2)
    step(pa, pb, snapshot[first + 1], 1)
    last(pb, snapshot[first], 0, 0)
    start(pa, "sources")
    step(pa, pb, snapshot[first + 6], 6)
    step(pb, pa, snapshot[first + 5], 5)
    last(pa, snapshot[first + 4], 4, 1)
    start(pa, "first")
    before = jnp.maximum(first - 4, 0)
    step(pa, pb, snapshot[before + 3], None)
    step(pb, pa, snapshot[before + 2], None)
    step(pa, pb, snapshot[before + 1], None)
    last(pb, snapshot[before], None, 2)


def first_inner(snapshot, guess, sources, velocity, res, base, edge_coef, own_vel, coarse_a, coarse_b, coef, pa, pb):
    t = lax.axis_index("tm")
    inner = (t > 0).astype(F32)
    zero = jnp.zeros((ROWS, LANE), F32)
    for buf in (pa, pb):
        buf[:, :LANE] = zero
        buf[:, PAD - LANE :] = zero
    for n in range(4):
        res[n, :, :LANE] = zero
        res[n, :, PAD - LANE :] = zero
        for c in range(4):
            coef[n, c, :, :LANE] = zero
            coef[n, c, :, PAD - LANE :] = zero
            edge_coef[n, c, :, :LANE] = zero[:16]
            edge_coef[n, c, :, PAD - LANE :] = zero[:16]

    for k in range(4):

        def build(c, carry):
            for r in range(0, ROWS, SUB):
                half = (0.5 * FINE_ADV) * velocity[k, c, r : r + SUB, :].astype(F32)
                for o, value in ((0, FINE_DIFF + half), (1, FINE_DIFF - half)):
                    coef[k, 2 * c + o, r : r + SUB, MID] = value
                    if r == 0:
                        edge_coef[k, 2 * c + o, SUB:, MID] = value
                    if r == ROWS - SUB:
                        edge_coef[k, 2 * c + o, :SUB, MID] = value
            return carry

        lax.fori_loop(0, 2, build, 0)
    at, left, right = chunk_at(t)
    half_lanes = lane_iota(ROWS) < 64
    for k in range(4):
        for c in range(2):
            own_vel[k, c, :, :CHUNK] = velocity[k, c, :, pl.ds(at, CHUNK)]
            x, y = velocity[k, c, :, pl.ds(right, LANE)], velocity[k, c, :, pl.ds(left, LANE)]
            own_vel[k, c, :, CHUNK:] = jnp.where(half_lanes, x.astype(F32), y.astype(F32)).astype(jnp.bfloat16)
    pack_coarse(own_vel, coarse_a, coarse_b)
    width = 1024

    def run(src, snap, use):
        def go(i, carry):
            l0 = i * width
            own = fine_step(src, lambda c, o, w: coef[snap, c, :, pl.ds(o, w)], l0, width)
            use(own, pl.ds(pl.multiple_of(l0, LANE), width), pl.ds(pl.multiple_of(l0 + LANE, LANE), width))
            return carry

        lax.fori_loop(0, COLS // width, go, 0)

    def step(src, dst, snap, source):
        def use(own, at, to):
            if source is not None:
                own = own + sources[source, :, at].astype(F32)
            dst[:, to] = own
            res[3, :, to] = res[3, :, to] + own

        run(src, snap, use)

    def last(src, snap, source, n):
        def use(own, at, to):
            if source is not None:
                own = own + sources[source, :, at].astype(F32)
                base[n, :, at] = own
                own = own - guess[n, :, at]
            res[n, :, to] = own

        run(src, snap, use)

    def start(buf, what):
        if what == "second":
            buf[:, MID] = guess[1]
        elif what == "sources":
            buf[:, MID] = sources[7].astype(F32)
        else:
            buf[:, MID] = guess[0] * inner

    res[3, :, MID] = guess[0] + guess[1] + sources[7].astype(F32)
    relax_chains(t, snapshot, step, last, start, pa, pb)


EDGE = 24


def first_edges(snapshot, guess, sources, in_a, in_b, inner_res, inner_base, edge_coef, pay, base, halo_coef, s_halo, pa, pb, acc, res):
    t = lax.axis_index("tm")
    s = lax.axis_index("space")
    odd = lax.rem(s, 2) == 1
    sub = sub_iota(COLS)
    low = sub < 4
    has_above = (s > 0).astype(F32)
    has_below = (s < lax.axis_size("space") - 1).astype(F32)
    inner = (t > 0).astype(F32)

    def tile(n):
        a = in_a[n * SUB : (n + 1) * SUB, :].astype(F32)
        b = in_b[n * SUB : (n + 1) * SUB, :].astype(F32)
        return jnp.where(odd, b, a), jnp.where(odd, a, b)

    def halves(n):
        below, above = tile(n)
        return jnp.where(low, below, roll4(above)), jnp.where(low, roll4(below), above)

    zero = jnp.zeros((EDGE, LANE), F32)
    for buf in (pa, pb):
        buf[:, :LANE] = zero
        buf[:, PAD - LANE :] = zero
    for k in range(4):
        pair = halves(k)
        for c in range(2):
            for n, value in coefficients(c, pair[c]):
                halo_coef[k, n, :, :LANE] = zero[:SUB]
                halo_coef[k, n, :, PAD - LANE :] = zero[:SUB]
                halo_coef[k, n, :, MID] = value
    g1, g0 = halves(4)
    s_halo[0], s_halo[4] = halves(5)
    below, above = tile(6)
    for i in range(4):
        x = pltpu.roll(below, 8 - 2 * i, 0) if i else below
        y = pltpu.roll(above, 6 - 2 * i, 0) if i < 3 else above
        s_halo[(2, 1, 6, 5)[i]] = jnp.where(sub < 2, x, jnp.where(sub >= 6, y, 0.0))
    s_halo[3] = s_halo[0]
    s_halo[7] = s_halo[4]

    width = 1024
    sub_w = sub_iota(width)
    edge = jnp.where(sub_w < 4, has_below, has_above)

    def run(src, snap, use):
        def coef(c, o, w):
            at = pl.ds(o, w)
            return jnp.concatenate(
                [edge_coef[snap, c, :SUB, at], halo_coef[snap, c, :, at], edge_coef[snap, c, SUB:, at]], 0
            )

        def go(i, carry):
            l0 = i * width
            out = fine_step(src, coef, l0, width)
            use(out, pl.ds(pl.multiple_of(l0, LANE), width), pl.ds(pl.multiple_of(l0 + LANE, LANE), width))
            return carry

        lax.fori_loop(0, COLS // width, go, 0)

    def tiles_of(source, at):
        return sources[source, ROWS - SUB :, at].astype(F32), sources[source, :SUB, at].astype(F32)

    def step(src, dst, snap, source):
        def use(out, at, to):
            x, h, y = out[:SUB], out[SUB : 2 * SUB] * edge, out[2 * SUB :]
            if source is not None:
                more = tiles_of(source, at)
                x, y = x + more[0], y + more[1]
                h = h + s_halo[source, :, at]
            dst[:SUB, to] = x
            dst[SUB : 2 * SUB, to] = h
            dst[2 * SUB :, to] = y
            acc[:SUB, at] = acc[:SUB, at] + x
            acc[SUB:, at] = acc[SUB:, at] + y

        run(src, snap, use)

    def last(src, snap, source, n):
        def use(out, at, to):
            x, y = out[:SUB], out[2 * SUB :]
            if source is not None:
                more = tiles_of(source, at)
                x, y = x + more[0], y + more[1]
                lo = sub_w < 4
                base[n, ROWS - SUB :, at] = jnp.where(lo, inner_base[n, ROWS - SUB :, at], x)
                base[n, :SUB, at] = jnp.where(lo, y, inner_base[n, :SUB, at])
                x = x - guess[n, ROWS - SUB :, at]
                y = y - guess[n, :SUB, at]
            res[n, :SUB, to] = x
            res[n, SUB:, to] = y

        run(src, snap, use)

    def start(buf, what):
        if what == "second":
            x, h, y = guess[1, ROWS - SUB :, :], g1, guess[1, :SUB, :]
        elif what == "sources":
            x, y = tiles_of(7, slice(None))
            h = s_halo[7]
        else:
            x, h, y = guess[0, ROWS - SUB :, :] * inner, g0 * inner, guess[0, :SUB, :] * inner
        buf[:SUB, MID] = x
        buf[SUB : 2 * SUB, MID] = h
        buf[2 * SUB :, MID] = y

    x7, y7 = tiles_of(7, slice(None))
    acc[:SUB, :] = guess[0, ROWS - SUB :, :] + guess[1, ROWS - SUB :, :] + x7
    acc[SUB:, :] = guess[0, :SUB, :] + guess[1, :SUB, :] + y7
    for n in range(4):
        res[n, :, :LANE] = zero[:16]
        res[n, :, PAD - LANE :] = zero[:16]
    for n in range(2):
        base[n, SUB : ROWS - SUB, :] = inner_base[n, SUB : ROWS - SUB, :]
    relax_chains(t, snapshot, step, last, start, pa, pb)
    res[3, :, MID] = acc[...]

    half = lane_iota(SUB) < 64
    lo = sub_iota(LANE) < 4

    def value(n, r, at):
        own = inner_res[n, r : r + SUB, at : at + LANE]
        if r == 0:
            return jnp.where(lo, res[n, SUB:, at : at + LANE], own)
        if r == ROWS - SUB:
            return jnp.where(lo, own, res[n, :SUB, at : at + LANE])
        return own

    for n in range(4):
        for r in range(0, ROWS, SUB):
            for d in range(NDEV):
                at = LANE + d * CHUNK
                for l in range(4):
                    pay[d, pl.ds(piece(n, l) + r, SUB), :] = value(n, r, at + l * LANE)
                if n < 3:
                    right, left = value(n, r, at + CHUNK), value(n, r, at - LANE)
                    pay[d, pl.ds(piece(n, 4) + r, SUB), :] = jnp.where(half, right, left)


PIECES = 19


def piece(n, l):
    return (5 * n + l) * ROWS


def field_rows(got, t, n, r, count):
    return jnp.concatenate([got[t, pl.ds(piece(n, l) + r, count), :] for l in range(5)], 1)


def level_rows(got, j, r):
    t, u = divmod(j, 2)
    value = field_rows(got, t, u, r, SUB)
    if u == 1 and t + 1 < NDEV:
        value = value + field_rows(got, t + 1, 2, r, SUB)
    return value


def pack_residual(got, out_a, out_b):
    odd = lax.rem(lax.axis_index("space"), 2) == 1
    n = 0
    for j, count in halo_tiles():
        for i in range(count):
            top, bottom = level_rows(got, j, 8 * i), level_rows(got, j, 24 - 8 * i)
            out_a[n * SUB : (n + 1) * SUB, :] = jnp.where(odd, top, bottom)
            out_b[n * SUB : (n + 1) * SUB, :] = jnp.where(odd, bottom, top)
            n += 1


def coarse_solve(snapshot, got, velocity, far_a, far_b, got_a, got_b, back, near, vnear, vel, res, mask):
    t = lax.axis_index("tm")
    s = lax.axis_index("space")
    odd = lax.rem(s, 2) == 1
    has_above = (s > 0).astype(F32)
    has_below = (s < lax.axis_size("space") - 1).astype(F32)
    has_left = (t > 0).astype(F32)
    has_right = (t < lax.axis_size("tm") - 1).astype(F32)
    row = lax.broadcasted_iota(jnp.int32, (FAR, WIDE), 0)
    col = lax.broadcasted_iota(jnp.int32, (FAR, WIDE), 1)
    in_rows = jnp.where(row < ROWS, 1.0, jnp.where(row < 52, has_below, has_above))
    in_cols = jnp.where(col < CHUNK, 1.0, jnp.where(col < CHUNK + 64, has_right, has_left))
    mask[...] = in_rows * in_cols

    sub = sub_iota(LANE)
    low = sub < 4

    def tile(n, l):
        at = (slice(n * SUB, (n + 1) * SUB), slice(l * LANE, (l + 1) * LANE))
        a, b = far_a[at].astype(F32), far_b[at].astype(F32)
        return jnp.where(odd, b, a), jnp.where(odd, a, b)

    coarse = 0.5 * COARSE_ADV
    for k in range(4):
        for c in range(2):
            for l in range(5):
                lanes = slice(l * LANE, (l + 1) * LANE)
                own = velocity[k, c, :, lanes].astype(F32)
                q = (k * 2 + c) * 2
                below0, above0 = tile(q, l)
                below1, above1 = tile(q + 1, l)
                edge = jnp.zeros((SUB, LANE), F32)
                if c == 0:
                    below, above = tile(16, l)
                    shifted = pltpu.roll(below, SUB - k, 0) if k else below
                    edge = jnp.where(sub == 0, shifted, edge)
                    edge = jnp.where(sub == 7, pltpu.roll(above, 7 - k, 0), edge)
                vel[k, c, :ROWS, lanes] = coarse * own
                vel[k, c, 32:40, lanes] = coarse * below0
                vel[k, c, 40:48, lanes] = coarse * below1
                vel[k, c, 48:56, lanes] = coarse * edge
                vel[k, c, 56:64, lanes] = coarse * above1
                vel[k, c, 64:72, lanes] = coarse * above0
                vnear[k, c, :ROWS, lanes] = velocity[k, c, :, lanes]
                vnear[k, c, ROWS:, lanes] = jnp.where(low, below0, above0).astype(jnp.bfloat16)

    n = 0
    low_w = sub_iota(WIDE) < 4
    empty = jnp.zeros((SUB, WIDE), F32)
    for j, count in halo_tiles():
        tiles = []
        for _ in range(count):
            a, b = got_a[n * SUB : (n + 1) * SUB, :], got_b[n * SUB : (n + 1) * SUB, :]
            tiles.append((jnp.where(odd, b, a), jnp.where(odd, a, b)))
            n += 1
        res[j, 32:40, :] = tiles[0][0]
        res[j, 64:72, :] = tiles[0][1]
        res[j, 40:48, :] = tiles[1][0] if count > 1 else empty
        res[j, 56:64, :] = tiles[1][1] if count > 1 else empty
        res[j, 48:56, :] = jnp.where(low_w, *tiles[2]) if count > 2 else empty
    res[0, ROWS:, :] = jnp.zeros((FAR - ROWS, WIDE), F32)
    for j in range(NCOARSE):
        res[j, :ROWS, :] = field_rows(got, j // 2, j % 2, 0, ROWS)

    for l in range(4):
        at = pl.ds(piece(3, l), ROWS)
        total = got[0, at, :]
        for d in range(1, NDEV):
            total = total + got[d, at, :]
        near[0, :ROWS, l * LANE : (l + 1) * LANE] = total

    def send(j, p, e):
        back[j // 2, j % 2] = e[:ROWS, :CHUNK]
        if j:
            near[j, :ROWS, :] = p[:ROWS]
            near[j, ROWS:, :] = jnp.where(low_w, p[32:40], p[64:72])
        near[0, :ROWS, :CHUNK] = near[0, :ROWS, :CHUNK] + p[:ROWS, :CHUNK]

    p = res[NCOARSE - 1]
    send(NCOARSE - 1, p, jnp.zeros_like(p))
    for j in range(NCOARSE - 2, -1, -1):
        snap = snapshot[4 * j]
        ax, ay = vel[snap, 0], vel[snap, 1]
        u = COARSE_DIFF * p
        wx = ax * p
        wy = ay * p
        e = (1.0 - 4.0 * COARSE_DIFF) * p + up(u + wx) + down(u - wx) + east(u + wy) + west(u - wy)
        e = e * mask[...]
        if j % 2 == 1:
            head = e[:ROWS] + field_rows(got, j // 2 + 1, 2, 0, ROWS)
            e = jnp.concatenate([head, e[ROWS:]], 0)
        p = e + res[j]
        send(j, p, e)


def second_relax(snapshot, near, vnear, grad, acc, coef):
    t = lax.axis_index("tm")
    s = lax.axis_index("space")
    has_above = (s > 0).astype(F32)
    has_below = (s < lax.axis_size("space") - 1).astype(F32)
    has_left = (t > 0).astype(F32)
    has_right = (t < lax.axis_size("tm") - 1).astype(F32)
    row = lax.broadcasted_iota(jnp.int32, (NEAR, WIDE), 0)
    col = lax.broadcasted_iota(jnp.int32, (NEAR, WIDE), 1)
    keep = (
        jnp.where(row == 0, has_above, 1.0),
        jnp.where(row == ROWS - 1, has_below, 1.0),
        jnp.where(col == 0, has_left, 1.0),
        jnp.where(col == CHUNK - 1, has_right, 1.0),
    )
    for k in range(4):
        for n in range(4):
            v = (0.5 * FINE_ADV) * vnear[k, n // 2].astype(F32)
            coef[k, n] = keep[n] * (FINE_DIFF - v if n % 2 else FINE_DIFF + v)
    acc[...] = near[0, :ROWS, :CHUNK]

    def interval(j):
        p = near[j + 1]
        total = None
        for k in (3, 2, 1):
            snap = snapshot[4 * j + k]
            c = [coef[snap, n] for n in range(4)]
            p = (1.0 - 4.0 * FINE_DIFF) * p + up(c[0] * p) + down(c[1] * p) + east(c[2] * p) + west(c[3] * p)
            own = p[:ROWS, :CHUNK]
            total = own if total is None else total + own
        return total

    def group(i, carry):
        total = interval(GROUP * i)
        for n in range(1, GROUP):
            total = total + interval(GROUP * i + n)
        acc[...] = acc[...] + total
        return carry

    lax.fori_loop(0, (NCOARSE - 1) // GROUP, group, 0)
    grad[...] = acc[...] * (1.0 / 64.0)


def finish(base, got, out):
    for d in range(NDEV):
        at = slice(d * CHUNK, (d + 1) * CHUNK)
        for u in range(2):
            out[u, :, at] = base[u, :, at] + got[d, u]


def cycle(guess, sources, velocity, snapshot):
    shape = jax.ShapeDtypeStruct
    bf = jnp.bfloat16
    packed = shape((FINE_TILES * SUB, COLS), bf)
    local = [shape(x.shape, x.dtype) for x in (guess, sources, velocity)]
    guess, sources, velocity = (pltpu.with_memory_space_constraint(x, pltpu.MemorySpace.HBM) for x in (guess, sources, velocity))
    fine_a, fine_b, guess, sources, velocity = call(
        pack_fine,
        (packed, packed, *local),
        (guess, sources, velocity),
        (pltpu.SemaphoreType.DMA((6,)),),
        vmem=12,
        space=pltpu.MemorySpace.HBM,
    )
    in_a, in_b = swap(fine_a, fine_b)
    field = lambda rows: pltpu.VMEM((rows, PAD), F32)
    coarse_rows = shape((COARSE_TILES * SUB, WIDE), bf)
    inner_res, inner_base, edge_coef, own_vel, coarse_a, coarse_b = call(
        first_inner,
        (
            shape((4, ROWS, PAD), F32),
            shape((2, ROWS, COLS), F32),
            shape((4, 4, 16, PAD), F32),
            shape((4, 2, ROWS, WIDE), bf),
            coarse_rows,
            coarse_rows,
        ),
        (snapshot, guess, sources, velocity),
        (pltpu.VMEM((4, 4, ROWS, PAD), F32), field(ROWS), field(ROWS)),
        vmem=24,
        flops=200_000_000,
    )
    far_a, far_b = swap(coarse_a, coarse_b)
    pay, base = call(
        first_edges,
        (shape((NDEV, PIECES * ROWS, LANE), F32), shape((2, ROWS, COLS), F32)),
        (snapshot, guess, sources, in_a, in_b, inner_res, inner_base, edge_coef),
        (
            pltpu.VMEM((4, 4, SUB, PAD), F32),
            pltpu.VMEM((8, SUB, COLS), F32),
            field(EDGE),
            field(EDGE),
            pltpu.VMEM((16, COLS), F32),
            pltpu.VMEM((4, 16, PAD), F32),
        ),
        vmem=20,
    )
    got = lax.all_to_all(pay.astype(LINK), "tm", 0, 0, tiled=False).astype(F32)
    tiles = sum(count for _, count in halo_tiles())
    edges = shape((tiles * SUB, WIDE), F32)
    send_a, send_b = call(pack_residual, (edges, edges), (got,), vmem=12)
    got_a, got_b = swap(send_a.astype(LINK), send_b.astype(LINK))
    back, near, vnear = call(
        coarse_solve,
        (
            shape((NDEV, 2, ROWS, CHUNK), F32),
            shape((NCOARSE, NEAR, WIDE), F32),
            shape((4, 2, NEAR, WIDE), bf),
        ),
        (snapshot, got, own_vel, far_a, far_b, got_a.astype(F32), got_b.astype(F32)),
        (
            pltpu.VMEM((4, 2, FAR, WIDE), F32),
            pltpu.VMEM((NCOARSE, FAR, WIDE), F32),
            pltpu.VMEM((FAR, WIDE), F32),
        ),
        vmem=20,
    )
    returned = lax.all_to_all(back.astype(LINK), "tm", 0, 0, tiled=False)
    grad = call(
        second_relax,
        shape((ROWS, CHUNK), F32),
        (snapshot, near, vnear),
        (pltpu.VMEM((ROWS, CHUNK), F32), pltpu.VMEM((4, 4, NEAR, WIDE), F32)),
        vmem=8,
    )
    c_values = call(finish, shape((2, ROWS, COLS), F32), (base, returned.astype(F32)), vmem=8)
    return c_values, grad


def solution(mesh):
    in_specs = (P("tm", "space", None), P("tm", "space", None), P(None, None, "space", None), P())
    out_specs = (P("tm", "space", None), P("space", "tm"))
    return jax.shard_map(cycle, mesh=mesh, in_specs=in_specs, out_specs=out_specs, check_vma=False)
```

```python
import jax
import jax.numpy as jnp
from jax import lax
from jax.experimental import pallas as pl
from jax.experimental.pallas import tpu as pltpu
from jax.sharding import PartitionSpec as P


FINE_DIFF = 0.2
FINE_ADV = 0.3
COARSE_DIFF = 0.24
COARSE_ADV = 0.4

F32 = jnp.float32
LINK = jnp.float16
LANE = 128
SUB = 8
ROWS = 32
COLS = 4096
CHUNK = 512
WIDE = 640
PAD = COLS + 2 * LANE
NEAR = 40
FAR = 72
NDEV = 8
NCOARSE = 16
GROUP = 3
MIB = 1024 * 1024

VM = pl.BlockSpec(memory_space=pltpu.VMEM)
SM = pl.BlockSpec(memory_space=pltpu.SMEM)


def halo_rows():
    parts = []
    for j in range(1, NCOARSE):
        for i, left in enumerate(range(j + 2, 0, -SUB)):
            parts.append((j, i, min(left, SUB)))
    parts.sort(key=lambda part: (-part[2], part[0]))
    tiles = []
    while parts:
        first = parts.pop(0)
        fits = [part for part in parts if part[2] + first[2] <= SUB]
        if fits:
            parts.remove(fits[0])
        tiles.append((first, *fits[:1]))
    return tiles


def call(kernel, outs, args, scratch=(), flops=10_000_000, vmem=16, space=pltpu.VMEM):
    specs = [SM if a.dtype == jnp.int32 else pl.BlockSpec(memory_space=space) for a in args]
    nbytes = sum(a.size * a.dtype.itemsize for a in args)
    return pl.pallas_call(
        kernel,
        out_shape=outs,
        in_specs=specs,
        out_specs=jax.tree.map(lambda _: VM, outs),
        scratch_shapes=list(scratch),
        compiler_params=pltpu.CompilerParams(vmem_limit_bytes=vmem * MIB),
        cost_estimate=pl.CostEstimate(flops=flops, bytes_accessed=nbytes, transcendentals=0),
    )(*args)


def sub_iota(cols):
    return lax.broadcasted_iota(jnp.int32, (SUB, cols), 0)


def lane_iota(rows):
    return lax.broadcasted_iota(jnp.int32, (rows, LANE), 1)


def roll4(x):
    return pltpu.roll(x, 4, 0)


def up(x):
    return pltpu.roll(x, x.shape[0] - 1, 0)


def down(x):
    return pltpu.roll(x, 1, 0)


def east(x):
    return pltpu.roll(x, x.shape[1] - 1, 1)


def west(x):
    return pltpu.roll(x, 1, 1)


def pack_fine(guess, sources, velocity, out_a, out_b, guess_v, sources_v, velocity_v, sems):
    odd = lax.rem(lax.axis_index("space"), 2) == 1
    copies = [pltpu.make_async_copy(velocity.at[k], velocity_v.at[k], sems.at[k]) for k in range(4)]
    copies.append(pltpu.make_async_copy(guess, guess_v, sems.at[4]))
    copies.append(pltpu.make_async_copy(sources, sources_v, sems.at[5]))
    for copy in copies:
        copy.start()
    first, final = slice(0, SUB), slice(ROWS - SUB, ROWS)
    vt, vb = velocity_v.at[:, :, first, :], velocity_v.at[:, :, final, :]
    st, sb = sources_v.at[:, first, :], sources_v.at[:, final, :]
    gt, gb = guess_v.at[:, first, :], guess_v.at[:, final, :]
    sub = sub_iota(COLS)
    low = sub < 4

    def put(n, top, bottom):
        out_a[n * SUB : (n + 1) * SUB, :] = jnp.where(odd, top, bottom).astype(jnp.bfloat16)
        out_b[n * SUB : (n + 1) * SUB, :] = jnp.where(odd, bottom, top).astype(jnp.bfloat16)

    def pair(n, x0, y0, x3, y3):
        put(n, jnp.where(low, x0, roll4(y0)), jnp.where(low, roll4(x3), y3))

    def turn(x, by):
        return pltpu.roll(x, by, 0) if by % SUB else x

    copies[4].wait()
    pair(4, gt[1], gt[0], gb[1], gb[0])
    copies[5].wait()
    for k in range(4):
        copies[k].wait()
        n, r = (2, 2, 6, 6)[k], k % 2
        x0, y0, x3, y3 = (ref[k, c].astype(F32) for ref in (vt, vb) for c in (0, 1))
        top = jnp.where(low, x0, roll4(y0))
        bottom = jnp.where(low, roll4(x3), y3)
        top = jnp.where(sub == 7, turn(st[n].astype(F32), 7 - r), top)
        bottom = jnp.where(sub == 4, turn(sb[n].astype(F32), 6 - r), bottom)
        put(k, top, bottom)
    top = jnp.where(low, st[3].astype(F32), roll4(st[7].astype(F32)))
    bottom = jnp.where(low, roll4(sb[3].astype(F32)), sb[7].astype(F32))
    top = jnp.where(sub == 3, turn(st[1].astype(F32), 3), jnp.where(sub == 7, turn(st[5].astype(F32), 7), top))
    bottom = jnp.where(sub == 0, turn(sb[1].astype(F32), 1), jnp.where(sub == 4, turn(sb[5].astype(F32), 5), bottom))
    put(5, top, bottom)


FINE_TILES = 6
COARSE_TILES = 17


def chunk_at(t):
    base = pl.multiple_of(t * CHUNK, LANE)
    left = pl.multiple_of(jnp.maximum(t * CHUNK - LANE, 0), LANE)
    right = pl.multiple_of(jnp.minimum(t * CHUNK + CHUNK, COLS - LANE), LANE)
    return base, left, right


def pack_coarse(velocity, out_a, out_b):
    odd = lax.rem(lax.axis_index("space"), 2) == 1
    sub = sub_iota(WIDE)
    wide = lambda k, c, r: velocity[k, c, r : r + SUB, :].astype(F32)

    def place(n, top, bottom):
        at = slice(n * SUB, (n + 1) * SUB)
        out_a[at, :] = jnp.where(odd, top, bottom).astype(jnp.bfloat16)
        out_b[at, :] = jnp.where(odd, bottom, top).astype(jnp.bfloat16)

    for k in range(4):
        for c in range(2):
            for i in range(2):
                place((k * 2 + c) * 2 + i, wide(k, c, 8 * i), wide(k, c, 24 - 8 * i))
    top = jnp.zeros((SUB, WIDE), F32)
    bottom = top
    for k in range(4):
        x, y = wide(k, 0, 16), wide(k, 0, 8)
        top = jnp.where(sub == k, pltpu.roll(x, k, 0) if k else x, top)
        bottom = jnp.where(sub == k, pltpu.roll(y, k + 1, 0), bottom)
    place(16, top, bottom)


def swap(buf_a, buf_b):
    count = lax.axis_size("space")
    pairs_b = [(i, i + 1) for i in range(1, count - 1, 2)]
    pairs_b = pairs_b + [(j, i) for i, j in pairs_b]
    pairs_a = [(i, i ^ 1) for i in range(count)]
    got_b = lax.ppermute(buf_b, "space", pairs_b)
    got_a = lax.ppermute(buf_a, "space", pairs_a)
    return got_a, got_b


MID = slice(LANE, PAD - LANE)


def fine_step(p, coef, l0, width):
    at = pl.multiple_of(l0, LANE)
    mid = pl.multiple_of(l0 + LANE, LANE)
    pc = p[:, pl.ds(mid, width)]
    out = (1.0 - 4.0 * FINE_DIFF) * pc
    out = out + up(coef(0, mid, width) * pc) + down(coef(1, mid, width) * pc)
    ge = coef(2, mid, width + LANE) * p[:, pl.ds(mid, width + LANE)]
    gw = coef(3, at, width + LANE) * p[:, pl.ds(at, width + LANE)]
    return out + east(ge)[:, :width] + west(gw)[:, LANE:]


def coefficients(c, v):
    half = 0.5 * FINE_ADV * v
    return ((2 * c, FINE_DIFF + half), (2 * c + 1, FINE_DIFF - half))


def relax_chains(t, snapshot, step, last, start, pa, pb):
    first = t * 8
    start(pa, "second")
    step(pa, pb, snapshot[first + 3], 3)
    step(pb, pa, snapshot[first + 2], 2)
    step(pa, pb, snapshot[first + 1], 1)
    last(pb, snapshot[first], 0, 0)
    start(pa, "sources")
    step(pa, pb, snapshot[first + 6], 6)
    step(pb, pa, snapshot[first + 5], 5)
    last(pa, snapshot[first + 4], 4, 1)
    start(pa, "first")
    before = jnp.maximum(first - 4, 0)
    step(pa, pb, snapshot[before + 3], None)
    step(pb, pa, snapshot[before + 2], None)
    step(pa, pb, snapshot[before + 1], None)
    last(pb, snapshot[before], None, 2)


def first_inner(snapshot, guess, sources, velocity, res, base, edge_coef, own_vel, coarse_a, coarse_b, coef, pa, pb):
    t = lax.axis_index("tm")
    inner = (t > 0).astype(F32)
    zero = jnp.zeros((ROWS, LANE), F32)
    for buf in (pa, pb):
        buf[:, :LANE] = zero
        buf[:, PAD - LANE :] = zero
    for n in range(4):
        res[n, :, :LANE] = zero
        res[n, :, PAD - LANE :] = zero
        for c in range(4):
            coef[n, c, :, :LANE] = zero
            coef[n, c, :, PAD - LANE :] = zero
            edge_coef[n, c, :, :LANE] = zero[:16]
            edge_coef[n, c, :, PAD - LANE :] = zero[:16]

    for k in range(4):

        def build(c, carry):
            for r in range(0, ROWS, SUB):
                half = (0.5 * FINE_ADV) * velocity[k, c, r : r + SUB, :].astype(F32)
                for o, value in ((0, FINE_DIFF + half), (1, FINE_DIFF - half)):
                    coef[k, 2 * c + o, r : r + SUB, MID] = value
                    if r == 0:
                        edge_coef[k, 2 * c + o, SUB:, MID] = value
                    if r == ROWS - SUB:
                        edge_coef[k, 2 * c + o, :SUB, MID] = value
            return carry

        lax.fori_loop(0, 2, build, 0)
    at, left, right = chunk_at(t)
    half_lanes = lane_iota(ROWS) < 64
    for k in range(4):
        for c in range(2):
            own_vel[k, c, :, :CHUNK] = velocity[k, c, :, pl.ds(at, CHUNK)]
            x, y = velocity[k, c, :, pl.ds(right, LANE)], velocity[k, c, :, pl.ds(left, LANE)]
            own_vel[k, c, :, CHUNK:] = jnp.where(half_lanes, x.astype(F32), y.astype(F32)).astype(jnp.bfloat16)
    pack_coarse(own_vel, coarse_a, coarse_b)
    width = 1024

    def run(src, snap, use):
        def go(i, carry):
            l0 = i * width
            own = fine_step(src, lambda c, o, w: coef[snap, c, :, pl.ds(o, w)], l0, width)
            use(own, pl.ds(pl.multiple_of(l0, LANE), width), pl.ds(pl.multiple_of(l0 + LANE, LANE), width))
            return carry

        lax.fori_loop(0, COLS // width, go, 0, unroll=True)

    def step(src, dst, snap, source):
        def use(own, at, to):
            if source is not None:
                own = own + sources[source, :, at].astype(F32)
            dst[:, to] = own
            res[3, :, to] = res[3, :, to] + own

        run(src, snap, use)

    def last(src, snap, source, n):
        def use(own, at, to):
            if source is not None:
                own = own + sources[source, :, at].astype(F32)
                base[n, :, at] = own
                own = own - guess[n, :, at]
            res[n, :, to] = own

        run(src, snap, use)

    def start(buf, what):
        if what == "second":
            buf[:, MID] = guess[1]
        elif what == "sources":
            buf[:, MID] = sources[7].astype(F32)
        else:
            buf[:, MID] = guess[0] * inner

    res[3, :, MID] = guess[0] + guess[1] + sources[7].astype(F32)
    relax_chains(t, snapshot, step, last, start, pa, pb)


EDGE = 24


def first_edges(snapshot, guess, sources, in_a, in_b, inner_res, inner_base, edge_coef, pay, base, halo_coef, s_halo, pa, pb, acc, res):
    t = lax.axis_index("tm")
    s = lax.axis_index("space")
    odd = lax.rem(s, 2) == 1
    sub = sub_iota(COLS)
    low = sub < 4
    has_above = (s > 0).astype(F32)
    has_below = (s < lax.axis_size("space") - 1).astype(F32)
    inner = (t > 0).astype(F32)

    def tile(n):
        a = in_a[n * SUB : (n + 1) * SUB, :].astype(F32)
        b = in_b[n * SUB : (n + 1) * SUB, :].astype(F32)
        return jnp.where(odd, b, a), jnp.where(odd, a, b)

    def halves(n):
        below, above = tile(n)
        return jnp.where(low, below, roll4(above)), jnp.where(low, roll4(below), above)

    zero = jnp.zeros((EDGE, LANE), F32)
    for buf in (pa, pb):
        buf[:, :LANE] = zero
        buf[:, PAD - LANE :] = zero
    for k in range(4):
        pair = halves(k)
        for c in range(2):
            for n, value in coefficients(c, pair[c]):
                halo_coef[k, n, :, :LANE] = zero[:SUB]
                halo_coef[k, n, :, PAD - LANE :] = zero[:SUB]
                halo_coef[k, n, :, MID] = value
    g1, g0 = halves(4)
    s_halo[3], s_halo[7] = halves(5)

    def turn(x, by):
        return pltpu.roll(x, by, 0) if by % SUB else x

    for n, k in ((2, 0), (6, 2)):
        (t0, b0), (t1, b1) = tile(k), tile(k + 1)
        value = jnp.where(sub == 0, turn(t0, 1), jnp.where(sub == 1, turn(t1, 2), 0.0))
        s_halo[n] = jnp.where(sub == 6, turn(b0, 2), jnp.where(sub == 7, turn(b1, 3), value))
    below, above = tile(5)
    for n, x, y in ((1, 5, 7), (5, 1, 3)):
        s_halo[n] = jnp.where(sub == 0, turn(below, x), jnp.where(sub == 7, turn(above, y), 0.0))

    width = 1024
    sub_w = sub_iota(width)
    edge = jnp.where(sub_w < 4, has_below, has_above)

    def run(src, snap, use):
        def coef(c, o, w):
            at = pl.ds(o, w)
            return jnp.concatenate(
                [edge_coef[snap, c, :SUB, at], halo_coef[snap, c, :, at], edge_coef[snap, c, SUB:, at]], 0
            )

        def go(i, carry):
            l0 = i * width
            out = fine_step(src, coef, l0, width)
            use(out, pl.ds(pl.multiple_of(l0, LANE), width), pl.ds(pl.multiple_of(l0 + LANE, LANE), width))
            return carry

        lax.fori_loop(0, COLS // width, go, 0, unroll=True)

    def tiles_of(source, at):
        return sources[source, ROWS - SUB :, at].astype(F32), sources[source, :SUB, at].astype(F32)

    def step(src, dst, snap, source):
        def use(out, at, to):
            x, h, y = out[:SUB], out[SUB : 2 * SUB] * edge, out[2 * SUB :]
            if source is not None:
                more = tiles_of(source, at)
                x, y = x + more[0], y + more[1]
                h = h + s_halo[source, :, at]
            dst[:SUB, to] = x
            dst[SUB : 2 * SUB, to] = h
            dst[2 * SUB :, to] = y
            acc[:SUB, at] = acc[:SUB, at] + x
            acc[SUB:, at] = acc[SUB:, at] + y

        run(src, snap, use)

    def last(src, snap, source, n):
        def use(out, at, to):
            x, y = out[:SUB], out[2 * SUB :]
            if source is not None:
                more = tiles_of(source, at)
                x, y = x + more[0], y + more[1]
                lo = sub_w < 4
                base[n, ROWS - SUB :, at] = jnp.where(lo, inner_base[n, ROWS - SUB :, at], x)
                base[n, :SUB, at] = jnp.where(lo, y, inner_base[n, :SUB, at])
                x = x - guess[n, ROWS - SUB :, at]
                y = y - guess[n, :SUB, at]
            res[n, :SUB, to] = x
            res[n, SUB:, to] = y

        run(src, snap, use)

    def start(buf, what):
        if what == "second":
            x, h, y = guess[1, ROWS - SUB :, :], g1, guess[1, :SUB, :]
        elif what == "sources":
            x, y = tiles_of(7, slice(None))
            h = s_halo[7]
        else:
            x, h, y = guess[0, ROWS - SUB :, :] * inner, g0 * inner, guess[0, :SUB, :] * inner
        buf[:SUB, MID] = x
        buf[SUB : 2 * SUB, MID] = h
        buf[2 * SUB :, MID] = y

    x7, y7 = tiles_of(7, slice(None))
    acc[:SUB, :] = guess[0, ROWS - SUB :, :] + guess[1, ROWS - SUB :, :] + x7
    acc[SUB:, :] = guess[0, :SUB, :] + guess[1, :SUB, :] + y7
    for n in range(4):
        res[n, :, :LANE] = zero[:16]
        res[n, :, PAD - LANE :] = zero[:16]
    for n in range(2):
        base[n, SUB : ROWS - SUB, :] = inner_base[n, SUB : ROWS - SUB, :]
    relax_chains(t, snapshot, step, last, start, pa, pb)
    res[3, :, MID] = acc[...]

    half = lane_iota(SUB) < 64
    lo = sub_iota(LANE) < 4

    def value(n, r, at):
        own = inner_res[n, r : r + SUB, at : at + LANE]
        if r == 0:
            return jnp.where(lo, res[n, SUB:, at : at + LANE], own)
        if r == ROWS - SUB:
            return jnp.where(lo, own, res[n, :SUB, at : at + LANE])
        return own

    for n in range(4):
        for r in range(0, ROWS, SUB):
            for d in range(NDEV):
                at = LANE + d * CHUNK
                for l in range(4):
                    pay[d, pl.ds(piece(n, l) + r, SUB), :] = value(n, r, at + l * LANE)
                if n < 3:
                    right, left = value(n, r, at + CHUNK), value(n, r, at - LANE)
                    pay[d, pl.ds(piece(n, 4) + r, SUB), :] = jnp.where(half, right, left)


PIECES = 19


def piece(n, l):
    return (5 * n + l) * ROWS


def field_rows(got, t, n, r, count):
    return jnp.concatenate([got[t, pl.ds(piece(n, l) + r, count), :] for l in range(5)], 1)


def level_rows(got, j, r):
    t, u = divmod(j, 2)
    value = field_rows(got, t, u, r, SUB)
    if u == 1 and t + 1 < NDEV:
        value = value + field_rows(got, t + 1, 2, r, SUB)
    return value


def pack_residual(got, out_a, out_b):
    odd = lax.rem(lax.axis_index("space"), 2) == 1
    sub = sub_iota(WIDE)
    for n, parts in enumerate(halo_rows()):
        (j, i, a), rest = parts[0], parts[1:]
        top, bottom = level_rows(got, j, SUB * i), level_rows(got, j, 24 - SUB * i)
        for j, i, _ in rest:
            top = jnp.where(sub < a, top, pltpu.roll(level_rows(got, j, SUB * i), a, 0))
            bottom = jnp.where(sub >= SUB - a, bottom, pltpu.roll(level_rows(got, j, 24 - SUB * i), SUB - a, 0))
        out_a[n * SUB : (n + 1) * SUB, :] = jnp.where(odd, top, bottom)
        out_b[n * SUB : (n + 1) * SUB, :] = jnp.where(odd, bottom, top)


def coarse_solve(snapshot, got, velocity, far_a, far_b, got_a, got_b, back, near, vnear, vel, res, mask):
    t = lax.axis_index("tm")
    s = lax.axis_index("space")
    odd = lax.rem(s, 2) == 1
    has_above = (s > 0).astype(F32)
    has_below = (s < lax.axis_size("space") - 1).astype(F32)
    has_left = (t > 0).astype(F32)
    has_right = (t < lax.axis_size("tm") - 1).astype(F32)
    row = lax.broadcasted_iota(jnp.int32, (FAR, WIDE), 0)
    col = lax.broadcasted_iota(jnp.int32, (FAR, WIDE), 1)
    in_rows = jnp.where(row < ROWS, 1.0, jnp.where(row < 52, has_below, has_above))
    in_cols = jnp.where(col < CHUNK, 1.0, jnp.where(col < CHUNK + 64, has_right, has_left))
    mask[...] = in_rows * in_cols

    sub = sub_iota(LANE)
    low = sub < 4

    def tile(n, l):
        at = (slice(n * SUB, (n + 1) * SUB), slice(l * LANE, (l + 1) * LANE))
        a, b = far_a[at].astype(F32), far_b[at].astype(F32)
        return jnp.where(odd, b, a), jnp.where(odd, a, b)

    coarse = 0.5 * COARSE_ADV
    for k in range(4):
        for c in range(2):
            for l in range(5):
                lanes = slice(l * LANE, (l + 1) * LANE)
                own = velocity[k, c, :, lanes].astype(F32)
                q = (k * 2 + c) * 2
                below0, above0 = tile(q, l)
                below1, above1 = tile(q + 1, l)
                edge = jnp.zeros((SUB, LANE), F32)
                if c == 0:
                    below, above = tile(16, l)
                    shifted = pltpu.roll(below, SUB - k, 0) if k else below
                    edge = jnp.where(sub == 0, shifted, edge)
                    edge = jnp.where(sub == 7, pltpu.roll(above, 7 - k, 0), edge)
                vel[k, c, :ROWS, lanes] = coarse * own
                vel[k, c, 32:40, lanes] = coarse * below0
                vel[k, c, 40:48, lanes] = coarse * below1
                vel[k, c, 48:56, lanes] = coarse * edge
                vel[k, c, 56:64, lanes] = coarse * above1
                vel[k, c, 64:72, lanes] = coarse * above0
                vnear[k, c, :ROWS, lanes] = velocity[k, c, :, lanes]
                vnear[k, c, ROWS:, lanes] = jnp.where(low, below0, above0).astype(jnp.bfloat16)

    low_w = sub_iota(WIDE) < 4
    empty = jnp.zeros((SUB, WIDE), F32)
    for j in range(1, NCOARSE):
        if j + 2 <= SUB:
            res[j, 40:48, :] = empty
            res[j, 56:64, :] = empty
        if j + 2 <= 2 * SUB:
            res[j, 48:56, :] = empty
    for n, parts in enumerate(halo_rows()):
        a, b = got_a[n * SUB : (n + 1) * SUB, :], got_b[n * SUB : (n + 1) * SUB, :]
        below, above = jnp.where(odd, b, a), jnp.where(odd, a, b)
        for m, (j, i, _) in enumerate(parts):
            if m:
                used = parts[0][2]
                below, above = pltpu.roll(below, SUB - used, 0), pltpu.roll(above, used, 0)
            if i == 2:
                res[j, 48:56, :] = jnp.where(low_w, below, above)
            else:
                res[j, 32 + SUB * i : 40 + SUB * i, :] = below
                res[j, 64 - SUB * i : 72 - SUB * i, :] = above
    res[0, ROWS:, :] = jnp.zeros((FAR - ROWS, WIDE), F32)
    for j in range(NCOARSE):
        res[j, :ROWS, :] = field_rows(got, j // 2, j % 2, 0, ROWS)

    for l in range(4):
        at = pl.ds(piece(3, l), ROWS)
        total = got[0, at, :]
        for d in range(1, NDEV):
            total = total + got[d, at, :]
        near[0, :ROWS, l * LANE : (l + 1) * LANE] = total

    def send(j, p, e):
        back[j // 2, j % 2] = e[:ROWS, :CHUNK]
        if j:
            near[j, :ROWS, :] = p[:ROWS]
            near[j, ROWS:, :] = jnp.where(low_w, p[32:40], p[64:72])
        near[0, :ROWS, :CHUNK] = near[0, :ROWS, :CHUNK] + p[:ROWS, :CHUNK]

    p = res[NCOARSE - 1]
    send(NCOARSE - 1, p, jnp.zeros_like(p))
    for j in range(NCOARSE - 2, -1, -1):
        snap = snapshot[4 * j]
        ax, ay = vel[snap, 0], vel[snap, 1]
        u = COARSE_DIFF * p
        wx = ax * p
        wy = ay * p
        e = (1.0 - 4.0 * COARSE_DIFF) * p + up(u + wx) + down(u - wx) + east(u + wy) + west(u - wy)
        e = e * mask[...]
        if j % 2 == 1:
            head = e[:ROWS] + field_rows(got, j // 2 + 1, 2, 0, ROWS)
            e = jnp.concatenate([head, e[ROWS:]], 0)
        p = e + res[j]
        send(j, p, e)


def second_relax(snapshot, near, vnear, grad, acc, coef):
    t = lax.axis_index("tm")
    s = lax.axis_index("space")
    has_above = (s > 0).astype(F32)
    has_below = (s < lax.axis_size("space") - 1).astype(F32)
    has_left = (t > 0).astype(F32)
    has_right = (t < lax.axis_size("tm") - 1).astype(F32)
    row = lax.broadcasted_iota(jnp.int32, (NEAR, WIDE), 0)
    col = lax.broadcasted_iota(jnp.int32, (NEAR, WIDE), 1)
    keep = (
        jnp.where(row == 0, has_above, 1.0),
        jnp.where(row == ROWS - 1, has_below, 1.0),
        jnp.where(col == 0, has_left, 1.0),
        jnp.where(col == CHUNK - 1, has_right, 1.0),
    )
    for k in range(4):
        for n in range(4):
            v = (0.5 * FINE_ADV) * vnear[k, n // 2].astype(F32)
            coef[k, n] = keep[n] * (FINE_DIFF - v if n % 2 else FINE_DIFF + v)
    acc[...] = near[0, :ROWS, :CHUNK]

    def interval(j):
        p = near[j + 1]
        total = None
        for k in (3, 2, 1):
            snap = snapshot[4 * j + k]
            c = [coef[snap, n] for n in range(4)]
            p = (1.0 - 4.0 * FINE_DIFF) * p + up(c[0] * p) + down(c[1] * p) + east(c[2] * p) + west(c[3] * p)
            own = p[:ROWS, :CHUNK]
            total = own if total is None else total + own
        return total

    def group(i, carry):
        total = interval(GROUP * i)
        for n in range(1, GROUP):
            total = total + interval(GROUP * i + n)
        acc[...] = acc[...] + total
        return carry

    lax.fori_loop(0, (NCOARSE - 1) // GROUP, group, 0)
    grad[...] = acc[...] * (1.0 / 64.0)


def finish(base, got, out):
    for d in range(NDEV):
        at = slice(d * CHUNK, (d + 1) * CHUNK)
        for u in range(2):
            out[u, :, at] = base[u, :, at] + got[d, u]


def cycle(guess, sources, velocity, snapshot):
    shape = jax.ShapeDtypeStruct
    bf = jnp.bfloat16
    packed = shape((FINE_TILES * SUB, COLS), bf)
    local = [shape(x.shape, x.dtype) for x in (guess, sources, velocity)]
    guess, sources, velocity = (pltpu.with_memory_space_constraint(x, pltpu.MemorySpace.HBM) for x in (guess, sources, velocity))
    fine_a, fine_b, guess, sources, velocity = call(
        pack_fine,
        (packed, packed, *local),
        (guess, sources, velocity),
        (pltpu.SemaphoreType.DMA((6,)),),
        vmem=12,
        space=pltpu.MemorySpace.HBM,
    )
    in_a, in_b = swap(fine_a, fine_b)
    field = lambda rows: pltpu.VMEM((rows, PAD), F32)
    coarse_rows = shape((COARSE_TILES * SUB, WIDE), bf)
    inner_res, inner_base, edge_coef, own_vel, coarse_a, coarse_b = call(
        first_inner,
        (
            shape((4, ROWS, PAD), F32),
            shape((2, ROWS, COLS), F32),
            shape((4, 4, 16, PAD), F32),
            shape((4, 2, ROWS, WIDE), bf),
            coarse_rows,
            coarse_rows,
        ),
        (snapshot, guess, sources, velocity),
        (pltpu.VMEM((4, 4, ROWS, PAD), F32), field(ROWS), field(ROWS)),
        vmem=24,
        flops=200_000_000,
    )
    far_a, far_b = swap(coarse_a, coarse_b)
    pay, base = call(
        first_edges,
        (shape((NDEV, PIECES * ROWS, LANE), F32), shape((2, ROWS, COLS), F32)),
        (snapshot, guess, sources, in_a, in_b, inner_res, inner_base, edge_coef),
        (
            pltpu.VMEM((4, 4, SUB, PAD), F32),
            pltpu.VMEM((8, SUB, COLS), F32),
            field(EDGE),
            field(EDGE),
            pltpu.VMEM((16, COLS), F32),
            pltpu.VMEM((4, 16, PAD), F32),
        ),
        vmem=20,
    )
    got = lax.all_to_all(pay.astype(LINK), "tm", 0, 0, tiled=False).astype(F32)
    tiles = len(halo_rows())
    edges = shape((tiles * SUB, WIDE), F32)
    send_a, send_b = call(pack_residual, (edges, edges), (got,), vmem=12)
    got_a, got_b = swap(send_a.astype(LINK), send_b.astype(LINK))
    back, near, vnear = call(
        coarse_solve,
        (
            shape((NDEV, 2, ROWS, CHUNK), F32),
            shape((NCOARSE, NEAR, WIDE), F32),
            shape((4, 2, NEAR, WIDE), bf),
        ),
        (snapshot, got, own_vel, far_a, far_b, got_a.astype(F32), got_b.astype(F32)),
        (
            pltpu.VMEM((4, 2, FAR, WIDE), F32),
            pltpu.VMEM((NCOARSE, FAR, WIDE), F32),
            pltpu.VMEM((FAR, WIDE), F32),
        ),
        vmem=20,
    )
    returned = lax.all_to_all(back.astype(LINK), "tm", 0, 0, tiled=False)
    grad = call(
        second_relax,
        shape((ROWS, CHUNK), F32),
        (snapshot, near, vnear),
        (pltpu.VMEM((ROWS, CHUNK), F32), pltpu.VMEM((4, 4, NEAR, WIDE), F32)),
        vmem=8,
    )
    c_values = call(finish, shape((2, ROWS, COLS), F32), (base, returned.astype(F32)), vmem=8)
    return c_values, grad


def solution(mesh):
    in_specs = (P("tm", "space", None), P("tm", "space", None), P(None, None, "space", None), P())
    out_specs = (P("tm", "space", None), P("space", "tm"))
    return jax.shard_map(cycle, mesh=mesh, in_specs=in_specs, out_specs=out_specs, check_vma=False)
```

```python
import jax
import jax.numpy as jnp
from jax import lax
from jax.experimental import pallas as pl
from jax.experimental.pallas import tpu as pltpu
from jax.sharding import PartitionSpec as P


FINE_DIFF = 0.2
FINE_ADV = 0.3
COARSE_DIFF = 0.24
COARSE_ADV = 0.4

F32 = jnp.float32
LINK = jnp.float16
LANE = 128
SUB = 8
ROWS = 32
COLS = 4096
CHUNK = 512
WIDE = 640
PAD = COLS + 2 * LANE
NEAR = 40
FAR = 72
NDEV = 8
NCOARSE = 16
GROUP = 3
MIB = 1024 * 1024

VM = pl.BlockSpec(memory_space=pltpu.VMEM)
SM = pl.BlockSpec(memory_space=pltpu.SMEM)


def halo_rows():
    parts = []
    for j in range(1, NCOARSE):
        for i, left in enumerate(range(j + 2, 0, -SUB)):
            parts.append((j, i, min(left, SUB)))
    parts.sort(key=lambda part: (-part[2], part[0]))
    tiles = []
    while parts:
        first = parts.pop(0)
        fits = [part for part in parts if part[2] + first[2] <= SUB]
        if fits:
            parts.remove(fits[0])
        tiles.append((first, *fits[:1]))
    return tiles


def call(kernel, outs, args, scratch=(), flops=10_000_000, vmem=16, space=pltpu.VMEM):
    specs = [SM if a.dtype == jnp.int32 else pl.BlockSpec(memory_space=space) for a in args]
    nbytes = sum(a.size * a.dtype.itemsize for a in args)
    return pl.pallas_call(
        kernel,
        out_shape=outs,
        in_specs=specs,
        out_specs=jax.tree.map(lambda _: VM, outs),
        scratch_shapes=list(scratch),
        compiler_params=pltpu.CompilerParams(vmem_limit_bytes=vmem * MIB),
        cost_estimate=pl.CostEstimate(flops=flops, bytes_accessed=nbytes, transcendentals=0),
    )(*args)


def sub_iota(cols):
    return lax.broadcasted_iota(jnp.int32, (SUB, cols), 0)


def lane_iota(rows):
    return lax.broadcasted_iota(jnp.int32, (rows, LANE), 1)


def roll4(x):
    return pltpu.roll(x, 4, 0)


def up(x):
    return pltpu.roll(x, x.shape[0] - 1, 0)


def down(x):
    return pltpu.roll(x, 1, 0)


def east(x):
    return pltpu.roll(x, x.shape[1] - 1, 1)


def west(x):
    return pltpu.roll(x, 1, 1)


def pack_fine(guess, sources, velocity, out_a, out_b, guess_v, sources_v, velocity_v, sems):
    odd = lax.rem(lax.axis_index("space"), 2) == 1
    copies = [pltpu.make_async_copy(velocity.at[k], velocity_v.at[k], sems.at[k]) for k in range(4)]
    copies.append(pltpu.make_async_copy(guess, guess_v, sems.at[4]))
    copies.append(pltpu.make_async_copy(sources, sources_v, sems.at[5]))
    for copy in copies:
        copy.start()
    first, final = slice(0, SUB), slice(ROWS - SUB, ROWS)
    vt, vb = velocity_v.at[:, :, first, :], velocity_v.at[:, :, final, :]
    st, sb = sources_v.at[:, first, :], sources_v.at[:, final, :]
    gt, gb = guess_v.at[:, first, :], guess_v.at[:, final, :]
    sub = sub_iota(COLS)
    low = sub < 4

    def put(n, top, bottom):
        out_a[n * SUB : (n + 1) * SUB, :] = jnp.where(odd, top, bottom).astype(jnp.bfloat16)
        out_b[n * SUB : (n + 1) * SUB, :] = jnp.where(odd, bottom, top).astype(jnp.bfloat16)

    def pair(n, x0, y0, x3, y3):
        put(n, jnp.where(low, x0, roll4(y0)), jnp.where(low, roll4(x3), y3))

    def turn(x, by):
        return pltpu.roll(x, by, 0) if by % SUB else x

    copies[4].wait()
    pair(4, gt[1], gt[0], gb[1], gb[0])
    copies[5].wait()
    for k in range(4):
        copies[k].wait()
        n, r = (2, 2, 6, 6)[k], k % 2
        x0, y0, x3, y3 = (ref[k, c].astype(F32) for ref in (vt, vb) for c in (0, 1))
        top = jnp.where(low, x0, roll4(y0))
        bottom = jnp.where(low, roll4(x3), y3)
        top = jnp.where(sub == 7, turn(st[n].astype(F32), 7 - r), top)
        bottom = jnp.where(sub == 4, turn(sb[n].astype(F32), 6 - r), bottom)
        put(k, top, bottom)
    top = jnp.where(low, st[3].astype(F32), roll4(st[7].astype(F32)))
    bottom = jnp.where(low, roll4(sb[3].astype(F32)), sb[7].astype(F32))
    top = jnp.where(sub == 3, turn(st[1].astype(F32), 3), jnp.where(sub == 7, turn(st[5].astype(F32), 7), top))
    bottom = jnp.where(sub == 0, turn(sb[1].astype(F32), 1), jnp.where(sub == 4, turn(sb[5].astype(F32), 5), bottom))
    put(5, top, bottom)


FINE_TILES = 6
COARSE_TILES = 17


def chunk_at(t):
    base = pl.multiple_of(t * CHUNK, LANE)
    left = pl.multiple_of(jnp.maximum(t * CHUNK - LANE, 0), LANE)
    right = pl.multiple_of(jnp.minimum(t * CHUNK + CHUNK, COLS - LANE), LANE)
    return base, left, right


def pack_coarse(velocity, out_a, out_b):
    odd = lax.rem(lax.axis_index("space"), 2) == 1
    sub = sub_iota(WIDE)
    wide = lambda k, c, r: velocity[k, c, r : r + SUB, :].astype(F32)

    def place(n, top, bottom):
        at = slice(n * SUB, (n + 1) * SUB)
        out_a[at, :] = jnp.where(odd, top, bottom).astype(jnp.bfloat16)
        out_b[at, :] = jnp.where(odd, bottom, top).astype(jnp.bfloat16)

    for k in range(4):
        for c in range(2):
            for i in range(2):
                place((k * 2 + c) * 2 + i, wide(k, c, 8 * i), wide(k, c, 24 - 8 * i))
    top = jnp.zeros((SUB, WIDE), F32)
    bottom = top
    for k in range(4):
        x, y = wide(k, 0, 16), wide(k, 0, 8)
        top = jnp.where(sub == k, pltpu.roll(x, k, 0) if k else x, top)
        bottom = jnp.where(sub == k, pltpu.roll(y, k + 1, 0), bottom)
    place(16, top, bottom)


def swap(buf_a, buf_b):
    count = lax.axis_size("space")
    pairs_b = [(i, i + 1) for i in range(1, count - 1, 2)]
    pairs_b = pairs_b + [(j, i) for i, j in pairs_b]
    pairs_a = [(i, i ^ 1) for i in range(count)]
    got_b = lax.ppermute(buf_b, "space", pairs_b)
    got_a = lax.ppermute(buf_a, "space", pairs_a)
    return got_a, got_b


MID = slice(LANE, PAD - LANE)


def fine_step(p, coef, l0, width):
    at = pl.multiple_of(l0, LANE)
    mid = pl.multiple_of(l0 + LANE, LANE)
    pc = p[:, pl.ds(mid, width)]
    out = (1.0 - 4.0 * FINE_DIFF) * pc
    out = out + up(coef(0, mid, width) * pc) + down(coef(1, mid, width) * pc)
    ge = coef(2, mid, width + LANE) * p[:, pl.ds(mid, width + LANE)]
    gw = coef(3, at, width + LANE) * p[:, pl.ds(at, width + LANE)]
    return out + east(ge)[:, :width] + west(gw)[:, LANE:]


def coefficients(c, v):
    half = 0.5 * FINE_ADV * v
    return ((2 * c, FINE_DIFF + half), (2 * c + 1, FINE_DIFF - half))


def relax_chains(t, snapshot, step, last, start, pa, pb):
    first = t * 8
    start(pa, "second")
    step(pa, pb, snapshot[first + 3], 3)
    step(pb, pa, snapshot[first + 2], 2)
    step(pa, pb, snapshot[first + 1], 1)
    last(pb, snapshot[first], 0, 0)
    start(pa, "sources")
    step(pa, pb, snapshot[first + 6], 6)
    step(pb, pa, snapshot[first + 5], 5)
    last(pa, snapshot[first + 4], 4, 1)
    start(pa, "first")
    before = jnp.maximum(first - 4, 0)
    step(pa, pb, snapshot[before + 3], None)
    step(pb, pa, snapshot[before + 2], None)
    step(pa, pb, snapshot[before + 1], None)
    last(pb, snapshot[before], None, 2)


def first_inner(snapshot, guess, sources, velocity, res, base, edge_coef, own_vel, coarse_a, coarse_b, coef, pa, pb):
    t = lax.axis_index("tm")
    inner = (t > 0).astype(F32)
    zero = jnp.zeros((ROWS, LANE), F32)
    for buf in (pa, pb):
        buf[:, :LANE] = zero
        buf[:, PAD - LANE :] = zero
    for n in range(4):
        res[n, :, :LANE] = zero
        res[n, :, PAD - LANE :] = zero
        for c in range(4):
            coef[n, c, :, :LANE] = zero
            coef[n, c, :, PAD - LANE :] = zero
            edge_coef[n, c, :, :LANE] = zero[:16]
            edge_coef[n, c, :, PAD - LANE :] = zero[:16]

    for k in range(4):

        def build(c, carry):
            for r in range(0, ROWS, SUB):
                half = (0.5 * FINE_ADV) * velocity[k, c, r : r + SUB, :].astype(F32)
                for o, value in ((0, FINE_DIFF + half), (1, FINE_DIFF - half)):
                    coef[k, 2 * c + o, r : r + SUB, MID] = value
                    if r == 0:
                        edge_coef[k, 2 * c + o, SUB:, MID] = value
                    if r == ROWS - SUB:
                        edge_coef[k, 2 * c + o, :SUB, MID] = value
            return carry

        lax.fori_loop(0, 2, build, 0)
    at, left, right = chunk_at(t)
    half_lanes = lane_iota(ROWS) < 64
    for k in range(4):
        for c in range(2):
            own_vel[k, c, :, :CHUNK] = velocity[k, c, :, pl.ds(at, CHUNK)]
            x, y = velocity[k, c, :, pl.ds(right, LANE)], velocity[k, c, :, pl.ds(left, LANE)]
            own_vel[k, c, :, CHUNK:] = jnp.where(half_lanes, x.astype(F32), y.astype(F32)).astype(jnp.bfloat16)
    pack_coarse(own_vel, coarse_a, coarse_b)
    width = 1024

    def run(src, snap, use):
        def go(i, carry):
            l0 = i * width
            own = fine_step(src, lambda c, o, w: coef[snap, c, :, pl.ds(o, w)], l0, width)
            use(own, pl.ds(pl.multiple_of(l0, LANE), width), pl.ds(pl.multiple_of(l0 + LANE, LANE), width))
            return carry

        lax.fori_loop(0, COLS // width, go, 0, unroll=True)

    def step(src, dst, snap, source):
        def use(own, at, to):
            if source is not None:
                own = own + sources[source, :, at].astype(F32)
            dst[:, to] = own
            res[3, :, to] = res[3, :, to] + own

        run(src, snap, use)

    def last(src, snap, source, n):
        def use(own, at, to):
            if source is not None:
                own = own + sources[source, :, at].astype(F32)
                base[n, :, at] = own
                own = own - guess[n, :, at]
            res[n, :, to] = own

        run(src, snap, use)

    def start(buf, what):
        if what == "second":
            buf[:, MID] = guess[1]
        elif what == "sources":
            buf[:, MID] = sources[7].astype(F32)
        else:
            buf[:, MID] = guess[0] * inner

    res[3, :, MID] = guess[0] + guess[1] + sources[7].astype(F32)
    relax_chains(t, snapshot, step, last, start, pa, pb)


EDGE = 24


def first_edges(snapshot, guess, sources, in_a, in_b, inner_res, inner_base, edge_coef, pay, base, halo_coef, s_halo, pa, pb, acc, res):
    t = lax.axis_index("tm")
    s = lax.axis_index("space")
    odd = lax.rem(s, 2) == 1
    sub = sub_iota(COLS)
    low = sub < 4
    has_above = (s > 0).astype(F32)
    has_below = (s < lax.axis_size("space") - 1).astype(F32)
    inner = (t > 0).astype(F32)

    def tile(n):
        a = in_a[n * SUB : (n + 1) * SUB, :].astype(F32)
        b = in_b[n * SUB : (n + 1) * SUB, :].astype(F32)
        return jnp.where(odd, b, a), jnp.where(odd, a, b)

    def halves(n):
        below, above = tile(n)
        return jnp.where(low, below, roll4(above)), jnp.where(low, roll4(below), above)

    zero = jnp.zeros((EDGE, LANE), F32)
    for buf in (pa, pb):
        buf[:, :LANE] = zero
        buf[:, PAD - LANE :] = zero
    for k in range(4):
        pair = halves(k)
        for c in range(2):
            for n, value in coefficients(c, pair[c]):
                halo_coef[k, n, :, :LANE] = zero[:SUB]
                halo_coef[k, n, :, PAD - LANE :] = zero[:SUB]
                halo_coef[k, n, :, MID] = value
    g1, g0 = halves(4)
    s_halo[3], s_halo[7] = halves(5)

    def turn(x, by):
        return pltpu.roll(x, by, 0) if by % SUB else x

    for n, k in ((2, 0), (6, 2)):
        (t0, b0), (t1, b1) = tile(k), tile(k + 1)
        value = jnp.where(sub == 0, turn(t0, 1), jnp.where(sub == 1, turn(t1, 2), 0.0))
        s_halo[n] = jnp.where(sub == 6, turn(b0, 2), jnp.where(sub == 7, turn(b1, 3), value))
    below, above = tile(5)
    for n, x, y in ((1, 5, 7), (5, 1, 3)):
        s_halo[n] = jnp.where(sub == 0, turn(below, x), jnp.where(sub == 7, turn(above, y), 0.0))

    width = 1024
    sub_w = sub_iota(width)
    edge = jnp.where(sub_w < 4, has_below, has_above)

    def run(src, snap, use):
        def coef(c, o, w):
            at = pl.ds(o, w)
            return jnp.concatenate(
                [edge_coef[snap, c, :SUB, at], halo_coef[snap, c, :, at], edge_coef[snap, c, SUB:, at]], 0
            )

        def go(i, carry):
            l0 = i * width
            out = fine_step(src, coef, l0, width)
            use(out, pl.ds(pl.multiple_of(l0, LANE), width), pl.ds(pl.multiple_of(l0 + LANE, LANE), width))
            return carry

        lax.fori_loop(0, COLS // width, go, 0, unroll=True)

    def tiles_of(source, at):
        return sources[source, ROWS - SUB :, at].astype(F32), sources[source, :SUB, at].astype(F32)

    def step(src, dst, snap, source):
        def use(out, at, to):
            x, h, y = out[:SUB], out[SUB : 2 * SUB] * edge, out[2 * SUB :]
            if source is not None:
                more = tiles_of(source, at)
                x, y = x + more[0], y + more[1]
                h = h + s_halo[source, :, at]
            dst[:SUB, to] = x
            dst[SUB : 2 * SUB, to] = h
            dst[2 * SUB :, to] = y
            acc[:SUB, at] = acc[:SUB, at] + x
            acc[SUB:, at] = acc[SUB:, at] + y

        run(src, snap, use)

    def last(src, snap, source, n):
        def use(out, at, to):
            x, y = out[:SUB], out[2 * SUB :]
            if source is not None:
                more = tiles_of(source, at)
                x, y = x + more[0], y + more[1]
                lo = sub_w < 4
                base[n, ROWS - SUB :, at] = jnp.where(lo, inner_base[n, ROWS - SUB :, at], x)
                base[n, :SUB, at] = jnp.where(lo, y, inner_base[n, :SUB, at])
                x = x - guess[n, ROWS - SUB :, at]
                y = y - guess[n, :SUB, at]
            res[n, :SUB, to] = x
            res[n, SUB:, to] = y

        run(src, snap, use)

    def start(buf, what):
        if what == "second":
            x, h, y = guess[1, ROWS - SUB :, :], g1, guess[1, :SUB, :]
        elif what == "sources":
            x, y = tiles_of(7, slice(None))
            h = s_halo[7]
        else:
            x, h, y = guess[0, ROWS - SUB :, :] * inner, g0 * inner, guess[0, :SUB, :] * inner
        buf[:SUB, MID] = x
        buf[SUB : 2 * SUB, MID] = h
        buf[2 * SUB :, MID] = y

    x7, y7 = tiles_of(7, slice(None))
    acc[:SUB, :] = guess[0, ROWS - SUB :, :] + guess[1, ROWS - SUB :, :] + x7
    acc[SUB:, :] = guess[0, :SUB, :] + guess[1, :SUB, :] + y7
    for n in range(4):
        res[n, :, :LANE] = zero[:16]
        res[n, :, PAD - LANE :] = zero[:16]
    for n in range(2):
        base[n, SUB : ROWS - SUB, :] = inner_base[n, SUB : ROWS - SUB, :]
    relax_chains(t, snapshot, step, last, start, pa, pb)
    res[3, :, MID] = acc[...]

    lane = lane_iota(SUB)
    lo = sub_iota(LANE) < 4

    def value(n, r, at):
        own = inner_res[n, r : r + SUB, at : at + LANE]
        if r == 0:
            return jnp.where(lo, res[n, SUB:, at : at + LANE], own)
        if r == ROWS - SUB:
            return jnp.where(lo, own, res[n, :SUB, at : at + LANE])
        return own

    for n in range(4):
        for r in range(0, ROWS, SUB):
            for d in range(NDEV):
                at = LANE + d * CHUNK
                for l in range(4):
                    pay[d, pl.ds(piece(n, l) + r, SUB), :] = value(n, r, at + l * LANE)

    def turn(x, by):
        return pltpu.roll(x, by % LANE, 1) if by % LANE else x

    for d in range(NDEV):
        at = LANE + d * CHUNK
        parts = []
        for q in range(12):
            n, r = divmod(q, 4)
            slot = 2 * HALO * (q % 3)
            parts.append(turn(value(n, SUB * r, at + CHUNK), slot))
            parts.append(turn(value(n, SUB * r, at - LANE), slot + 2 * HALO))
        for m in range(4):
            packed = parts[6 * m + 5]
            for k in range(4, -1, -1):
                packed = jnp.where(lane < HALO * (k + 1), parts[6 * m + k], packed)
            pay[d, pl.ds(piece(4, 0) + SUB * m, SUB), :] = packed


HALO = 20
PIECES = 17


def piece(n, l):
    return (4 * n + l) * ROWS


def halo_columns(got, t, n, r):
    m, slot = divmod(4 * n + r // SUB, 3)
    x = got[t, pl.ds(piece(4, 0) + SUB * m, SUB), :]
    right = pltpu.roll(x, LANE - 2 * HALO * slot, 1) if slot else x
    left = pltpu.roll(x, (2 * LANE - 2 * HALO * (slot + 1)) % LANE, 1)
    return jnp.where(lane_iota(SUB) < 64, right, left)


def field_rows(got, t, n, r, count):
    last = jnp.concatenate([halo_columns(got, t, n, r + i) for i in range(0, count, SUB)], 0)
    return jnp.concatenate([*(got[t, pl.ds(piece(n, l) + r, count), :] for l in range(4)), last], 1)


def level_rows(got, j, r):
    t, u = divmod(j, 2)
    value = field_rows(got, t, u, r, SUB)
    if u == 1 and t + 1 < NDEV:
        value = value + field_rows(got, t + 1, 2, r, SUB)
    return value


def pack_residual(got, out_a, out_b):
    odd = lax.rem(lax.axis_index("space"), 2) == 1
    sub = sub_iota(WIDE)
    for n, parts in enumerate(halo_rows()):
        (j, i, a), rest = parts[0], parts[1:]
        top, bottom = level_rows(got, j, SUB * i), level_rows(got, j, 24 - SUB * i)
        for j, i, _ in rest:
            top = jnp.where(sub < a, top, pltpu.roll(level_rows(got, j, SUB * i), a, 0))
            bottom = jnp.where(sub >= SUB - a, bottom, pltpu.roll(level_rows(got, j, 24 - SUB * i), SUB - a, 0))
        out_a[n * SUB : (n + 1) * SUB, :] = jnp.where(odd, top, bottom)
        out_b[n * SUB : (n + 1) * SUB, :] = jnp.where(odd, bottom, top)


def coarse_solve(snapshot, got, velocity, far_a, far_b, got_a, got_b, back, near, vnear, vel, res, mask):
    t = lax.axis_index("tm")
    s = lax.axis_index("space")
    odd = lax.rem(s, 2) == 1
    has_above = (s > 0).astype(F32)
    has_below = (s < lax.axis_size("space") - 1).astype(F32)
    has_left = (t > 0).astype(F32)
    has_right = (t < lax.axis_size("tm") - 1).astype(F32)
    row = lax.broadcasted_iota(jnp.int32, (FAR, WIDE), 0)
    col = lax.broadcasted_iota(jnp.int32, (FAR, WIDE), 1)
    in_rows = jnp.where(row < ROWS, 1.0, jnp.where(row < 52, has_below, has_above))
    in_cols = jnp.where(col < CHUNK, 1.0, jnp.where(col < CHUNK + 64, has_right, has_left))
    mask[...] = in_rows * in_cols

    sub = sub_iota(LANE)
    low = sub < 4

    def tile(n, l):
        at = (slice(n * SUB, (n + 1) * SUB), slice(l * LANE, (l + 1) * LANE))
        a, b = far_a[at].astype(F32), far_b[at].astype(F32)
        return jnp.where(odd, b, a), jnp.where(odd, a, b)

    coarse = 0.5 * COARSE_ADV
    for k in range(4):
        for c in range(2):
            for l in range(5):
                lanes = slice(l * LANE, (l + 1) * LANE)
                own = velocity[k, c, :, lanes].astype(F32)
                q = (k * 2 + c) * 2
                below0, above0 = tile(q, l)
                below1, above1 = tile(q + 1, l)
                edge = jnp.zeros((SUB, LANE), F32)
                if c == 0:
                    below, above = tile(16, l)
                    shifted = pltpu.roll(below, SUB - k, 0) if k else below
                    edge = jnp.where(sub == 0, shifted, edge)
                    edge = jnp.where(sub == 7, pltpu.roll(above, 7 - k, 0), edge)
                vel[k, c, :ROWS, lanes] = coarse * own
                vel[k, c, 32:40, lanes] = coarse * below0
                vel[k, c, 40:48, lanes] = coarse * below1
                vel[k, c, 48:56, lanes] = coarse * edge
                vel[k, c, 56:64, lanes] = coarse * above1
                vel[k, c, 64:72, lanes] = coarse * above0
                vnear[k, c, :ROWS, lanes] = velocity[k, c, :, lanes]
                vnear[k, c, ROWS:, lanes] = jnp.where(low, below0, above0).astype(jnp.bfloat16)

    low_w = sub_iota(WIDE) < 4
    empty = jnp.zeros((SUB, WIDE), F32)
    for j in range(1, NCOARSE):
        if j + 2 <= SUB:
            res[j, 40:48, :] = empty
            res[j, 56:64, :] = empty
        if j + 2 <= 2 * SUB:
            res[j, 48:56, :] = empty
    for n, parts in enumerate(halo_rows()):
        a, b = got_a[n * SUB : (n + 1) * SUB, :], got_b[n * SUB : (n + 1) * SUB, :]
        below, above = jnp.where(odd, b, a), jnp.where(odd, a, b)
        for m, (j, i, _) in enumerate(parts):
            if m:
                used = parts[0][2]
                below, above = pltpu.roll(below, SUB - used, 0), pltpu.roll(above, used, 0)
            if i == 2:
                res[j, 48:56, :] = jnp.where(low_w, below, above)
            else:
                res[j, 32 + SUB * i : 40 + SUB * i, :] = below
                res[j, 64 - SUB * i : 72 - SUB * i, :] = above
    res[0, ROWS:, :] = jnp.zeros((FAR - ROWS, WIDE), F32)
    for j in range(NCOARSE):
        res[j, :ROWS, :] = field_rows(got, j // 2, j % 2, 0, ROWS)

    for l in range(4):
        at = pl.ds(piece(3, l), ROWS)
        total = got[0, at, :]
        for d in range(1, NDEV):
            total = total + got[d, at, :]
        near[0, :ROWS, l * LANE : (l + 1) * LANE] = total

    def send(j, p, e):
        back[j // 2, j % 2] = e[:ROWS, :CHUNK]
        if j:
            near[j, :ROWS, :] = p[:ROWS]
            near[j, ROWS:, :] = jnp.where(low_w, p[32:40], p[64:72])
        near[0, :ROWS, :CHUNK] = near[0, :ROWS, :CHUNK] + p[:ROWS, :CHUNK]

    p = res[NCOARSE - 1]
    send(NCOARSE - 1, p, jnp.zeros_like(p))
    for j in range(NCOARSE - 2, -1, -1):
        snap = snapshot[4 * j]
        ax, ay = vel[snap, 0], vel[snap, 1]
        u = COARSE_DIFF * p
        wx = ax * p
        wy = ay * p
        e = (1.0 - 4.0 * COARSE_DIFF) * p + up(u + wx) + down(u - wx) + east(u + wy) + west(u - wy)
        e = e * mask[...]
        if j % 2 == 1:
            head = e[:ROWS] + field_rows(got, j // 2 + 1, 2, 0, ROWS)
            e = jnp.concatenate([head, e[ROWS:]], 0)
        p = e + res[j]
        send(j, p, e)


def second_relax(snapshot, near, vnear, grad, acc, coef):
    t = lax.axis_index("tm")
    s = lax.axis_index("space")
    has_above = (s > 0).astype(F32)
    has_below = (s < lax.axis_size("space") - 1).astype(F32)
    has_left = (t > 0).astype(F32)
    has_right = (t < lax.axis_size("tm") - 1).astype(F32)
    row = lax.broadcasted_iota(jnp.int32, (NEAR, WIDE), 0)
    col = lax.broadcasted_iota(jnp.int32, (NEAR, WIDE), 1)
    keep = (
        jnp.where(row == 0, has_above, 1.0),
        jnp.where(row == ROWS - 1, has_below, 1.0),
        jnp.where(col == 0, has_left, 1.0),
        jnp.where(col == CHUNK - 1, has_right, 1.0),
    )
    for k in range(4):
        for n in range(4):
            v = (0.5 * FINE_ADV) * vnear[k, n // 2].astype(F32)
            coef[k, n] = keep[n] * (FINE_DIFF - v if n % 2 else FINE_DIFF + v)
    acc[...] = near[0, :ROWS, :CHUNK]

    def interval(j):
        p = near[j + 1]
        total = None
        for k in (3, 2, 1):
            snap = snapshot[4 * j + k]
            c = [coef[snap, n] for n in range(4)]
            p = (1.0 - 4.0 * FINE_DIFF) * p + up(c[0] * p) + down(c[1] * p) + east(c[2] * p) + west(c[3] * p)
            own = p[:ROWS, :CHUNK]
            total = own if total is None else total + own
        return total

    def group(i, carry):
        total = interval(GROUP * i)
        for n in range(1, GROUP):
            total = total + interval(GROUP * i + n)
        acc[...] = acc[...] + total
        return carry

    lax.fori_loop(0, (NCOARSE - 1) // GROUP, group, 0)
    grad[...] = acc[...] * (1.0 / 64.0)


def finish(base, got, out):
    for d in range(NDEV):
        at = slice(d * CHUNK, (d + 1) * CHUNK)
        for u in range(2):
            out[u, :, at] = base[u, :, at] + got[d, u]


def cycle(guess, sources, velocity, snapshot):
    shape = jax.ShapeDtypeStruct
    bf = jnp.bfloat16
    packed = shape((FINE_TILES * SUB, COLS), bf)
    local = [shape(x.shape, x.dtype) for x in (guess, sources, velocity)]
    guess, sources, velocity = (pltpu.with_memory_space_constraint(x, pltpu.MemorySpace.HBM) for x in (guess, sources, velocity))
    fine_a, fine_b, guess, sources, velocity = call(
        pack_fine,
        (packed, packed, *local),
        (guess, sources, velocity),
        (pltpu.SemaphoreType.DMA((6,)),),
        vmem=12,
        space=pltpu.MemorySpace.HBM,
    )
    in_a, in_b = swap(fine_a, fine_b)
    field = lambda rows: pltpu.VMEM((rows, PAD), F32)
    coarse_rows = shape((COARSE_TILES * SUB, WIDE), bf)
    inner_res, inner_base, edge_coef, own_vel, coarse_a, coarse_b = call(
        first_inner,
        (
            shape((4, ROWS, PAD), F32),
            shape((2, ROWS, COLS), F32),
            shape((4, 4, 16, PAD), F32),
            shape((4, 2, ROWS, WIDE), bf),
            coarse_rows,
            coarse_rows,
        ),
        (snapshot, guess, sources, velocity),
        (pltpu.VMEM((4, 4, ROWS, PAD), F32), field(ROWS), field(ROWS)),
        vmem=24,
        flops=200_000_000,
    )
    far_a, far_b = swap(coarse_a, coarse_b)
    pay, base = call(
        first_edges,
        (shape((NDEV, PIECES * ROWS, LANE), F32), shape((2, ROWS, COLS), F32)),
        (snapshot, guess, sources, in_a, in_b, inner_res, inner_base, edge_coef),
        (
            pltpu.VMEM((4, 4, SUB, PAD), F32),
            pltpu.VMEM((8, SUB, COLS), F32),
            field(EDGE),
            field(EDGE),
            pltpu.VMEM((16, COLS), F32),
            pltpu.VMEM((4, 16, PAD), F32),
        ),
        vmem=20,
    )
    got = lax.all_to_all(pay.astype(LINK), "tm", 0, 0, tiled=False).astype(F32)
    tiles = len(halo_rows())
    edges = shape((tiles * SUB, WIDE), F32)
    send_a, send_b = call(pack_residual, (edges, edges), (got,), vmem=12)
    got_a, got_b = swap(send_a.astype(LINK), send_b.astype(LINK))
    back, near, vnear = call(
        coarse_solve,
        (
            shape((NDEV, 2, ROWS, CHUNK), F32),
            shape((NCOARSE, NEAR, WIDE), F32),
            shape((4, 2, NEAR, WIDE), bf),
        ),
        (snapshot, got, own_vel, far_a, far_b, got_a.astype(F32), got_b.astype(F32)),
        (
            pltpu.VMEM((4, 2, FAR, WIDE), F32),
            pltpu.VMEM((NCOARSE, FAR, WIDE), F32),
            pltpu.VMEM((FAR, WIDE), F32),
        ),
        vmem=20,
    )
    returned = lax.all_to_all(back.astype(LINK), "tm", 0, 0, tiled=False)
    grad = call(
        second_relax,
        shape((ROWS, CHUNK), F32),
        (snapshot, near, vnear),
        (pltpu.VMEM((ROWS, CHUNK), F32), pltpu.VMEM((4, 4, NEAR, WIDE), F32)),
        vmem=8,
    )
    c_values = call(finish, shape((2, ROWS, COLS), F32), (base, returned.astype(F32)), vmem=8)
    return c_values, grad


def solution(mesh):
    in_specs = (P("tm", "space", None), P("tm", "space", None), P(None, None, "space", None), P())
    out_specs = (P("tm", "space", None), P("space", "tm"))
    return jax.shard_map(cycle, mesh=mesh, in_specs=in_specs, out_specs=out_specs, check_vma=False)
```

```python
import jax
import jax.numpy as jnp
from jax import lax
from jax.experimental import pallas as pl
from jax.experimental.pallas import tpu as pltpu
from jax.sharding import PartitionSpec as P


FINE_DIFF = 0.2
FINE_ADV = 0.3
COARSE_DIFF = 0.24
COARSE_ADV = 0.4

F32 = jnp.float32
LINK = jnp.float16
LANE = 128
SUB = 8
ROWS = 32
COLS = 4096
CHUNK = 512
WIDE = 640
PAD = COLS + 2 * LANE
NEAR = 40
FAR = 72
NDEV = 8
NCOARSE = 16
GROUP = 3
MIB = 1024 * 1024

VM = pl.BlockSpec(memory_space=pltpu.VMEM)
SM = pl.BlockSpec(memory_space=pltpu.SMEM)


def halo_rows():
    parts = []
    for j in range(1, NCOARSE):
        for i, left in enumerate(range(j + 2, 0, -SUB)):
            parts.append((j, i, min(left, SUB)))
    parts.sort(key=lambda part: (-part[2], part[0]))
    tiles = []
    while parts:
        first = parts.pop(0)
        fits = [part for part in parts if part[2] + first[2] <= SUB]
        if fits:
            parts.remove(fits[0])
        tiles.append((first, *fits[:1]))
    return tiles


def call(kernel, outs, args, scratch=(), flops=10_000_000, vmem=16, space=pltpu.VMEM):
    specs = [SM if a.dtype == jnp.int32 else pl.BlockSpec(memory_space=space) for a in args]
    nbytes = sum(a.size * a.dtype.itemsize for a in args)
    return pl.pallas_call(
        kernel,
        out_shape=outs,
        in_specs=specs,
        out_specs=jax.tree.map(lambda _: VM, outs),
        scratch_shapes=list(scratch),
        compiler_params=pltpu.CompilerParams(vmem_limit_bytes=vmem * MIB),
        cost_estimate=pl.CostEstimate(flops=flops, bytes_accessed=nbytes, transcendentals=0),
    )(*args)


def sub_iota(cols):
    return lax.broadcasted_iota(jnp.int32, (SUB, cols), 0)


def lane_iota(rows):
    return lax.broadcasted_iota(jnp.int32, (rows, LANE), 1)


def roll4(x):
    return pltpu.roll(x, 4, 0)


def up(x):
    return pltpu.roll(x, x.shape[0] - 1, 0)


def down(x):
    return pltpu.roll(x, 1, 0)


def east(x):
    return pltpu.roll(x, x.shape[1] - 1, 1)


def west(x):
    return pltpu.roll(x, 1, 1)


def pack_fine(guess, sources, velocity, out_a, out_b, guess_v, sources_v, velocity_v, sems):
    odd = lax.rem(lax.axis_index("space"), 2) == 1
    copies = [pltpu.make_async_copy(velocity.at[k], velocity_v.at[k], sems.at[k]) for k in range(4)]
    copies.append(pltpu.make_async_copy(guess, guess_v, sems.at[4]))
    copies += [pltpu.make_async_copy(sources.at[n], sources_v.at[n], sems.at[5 + n]) for n in range(8)]
    for copy in copies:
        copy.start()
    first, final = slice(0, SUB), slice(ROWS - SUB, ROWS)
    vt, vb = velocity_v.at[:, :, first, :], velocity_v.at[:, :, final, :]
    st, sb = sources_v.at[:, first, :], sources_v.at[:, final, :]
    gt, gb = guess_v.at[:, first, :], guess_v.at[:, final, :]
    sub = sub_iota(COLS)
    low = sub < 4

    def put(n, top, bottom):
        out_a[n * SUB : (n + 1) * SUB, :] = jnp.where(odd, top, bottom).astype(jnp.bfloat16)
        out_b[n * SUB : (n + 1) * SUB, :] = jnp.where(odd, bottom, top).astype(jnp.bfloat16)

    def pair(n, x0, y0, x3, y3):
        put(n, jnp.where(low, x0, roll4(y0)), jnp.where(low, roll4(x3), y3))

    def turn(x, by):
        return pltpu.roll(x, by, 0) if by % SUB else x

    copies[4].wait()
    pair(4, gt[1], gt[0], gb[1], gb[0])
    for copy in copies[5:]:
        copy.wait()
    for k in range(4):
        copies[k].wait()
        n, r = (2, 2, 6, 6)[k], k % 2
        x0, y0, x3, y3 = (ref[k, c].astype(F32) for ref in (vt, vb) for c in (0, 1))
        top = jnp.where(low, x0, roll4(y0))
        bottom = jnp.where(low, roll4(x3), y3)
        top = jnp.where(sub == 7, turn(st[n].astype(F32), 7 - r), top)
        bottom = jnp.where(sub == 4, turn(sb[n].astype(F32), 6 - r), bottom)
        put(k, top, bottom)
    top = jnp.where(low, st[3].astype(F32), roll4(st[7].astype(F32)))
    bottom = jnp.where(low, roll4(sb[3].astype(F32)), sb[7].astype(F32))
    top = jnp.where(sub == 3, turn(st[1].astype(F32), 3), jnp.where(sub == 7, turn(st[5].astype(F32), 7), top))
    bottom = jnp.where(sub == 0, turn(sb[1].astype(F32), 1), jnp.where(sub == 4, turn(sb[5].astype(F32), 5), bottom))
    put(5, top, bottom)


FINE_TILES = 6
COARSE_TILES = 17


def chunk_at(t):
    base = pl.multiple_of(t * CHUNK, LANE)
    left = pl.multiple_of(jnp.maximum(t * CHUNK - LANE, 0), LANE)
    right = pl.multiple_of(jnp.minimum(t * CHUNK + CHUNK, COLS - LANE), LANE)
    return base, left, right


def pack_coarse(velocity, out_a, out_b):
    odd = lax.rem(lax.axis_index("space"), 2) == 1
    sub = sub_iota(WIDE)
    wide = lambda k, c, r: velocity[k, c, r : r + SUB, :].astype(F32)

    def place(n, top, bottom):
        at = slice(n * SUB, (n + 1) * SUB)
        out_a[at, :] = jnp.where(odd, top, bottom).astype(jnp.bfloat16)
        out_b[at, :] = jnp.where(odd, bottom, top).astype(jnp.bfloat16)

    for k in range(4):
        for c in range(2):
            for i in range(2):
                place((k * 2 + c) * 2 + i, wide(k, c, 8 * i), wide(k, c, 24 - 8 * i))
    top = jnp.zeros((SUB, WIDE), F32)
    bottom = top
    for k in range(4):
        x, y = wide(k, 0, 16), wide(k, 0, 8)
        top = jnp.where(sub == k, pltpu.roll(x, k, 0) if k else x, top)
        bottom = jnp.where(sub == k, pltpu.roll(y, k + 1, 0), bottom)
    place(16, top, bottom)


def swap(buf_a, buf_b):
    count = lax.axis_size("space")
    pairs_b = [(i, i + 1) for i in range(1, count - 1, 2)]
    pairs_b = pairs_b + [(j, i) for i, j in pairs_b]
    pairs_a = [(i, i ^ 1) for i in range(count)]
    got_b = lax.ppermute(buf_b, "space", pairs_b)
    got_a = lax.ppermute(buf_a, "space", pairs_a)
    return got_a, got_b


MID = slice(LANE, PAD - LANE)


def fine_step(p, coef, l0, width):
    at = pl.multiple_of(l0, LANE)
    mid = pl.multiple_of(l0 + LANE, LANE)
    pc = p[:, pl.ds(mid, width)]
    out = (1.0 - 4.0 * FINE_DIFF) * pc
    out = out + up(coef(0, mid, width) * pc) + down(coef(1, mid, width) * pc)
    ge = coef(2, mid, width + LANE) * p[:, pl.ds(mid, width + LANE)]
    gw = coef(3, at, width + LANE) * p[:, pl.ds(at, width + LANE)]
    return out + east(ge)[:, :width] + west(gw)[:, LANE:]


def coefficients(c, v):
    half = 0.5 * FINE_ADV * v
    return ((2 * c, FINE_DIFF + half), (2 * c + 1, FINE_DIFF - half))


def relax_chains(t, snapshot, step, last, start, pa, pb):
    first = t * 8
    start(pa, "second")
    step(pa, pb, snapshot[first + 3], 3)
    step(pb, pa, snapshot[first + 2], 2)
    step(pa, pb, snapshot[first + 1], 1)
    last(pb, snapshot[first], 0, 0)
    start(pa, "sources")
    step(pa, pb, snapshot[first + 6], 6)
    step(pb, pa, snapshot[first + 5], 5)
    last(pa, snapshot[first + 4], 4, 1)
    start(pa, "first")
    before = jnp.maximum(first - 4, 0)
    step(pa, pb, snapshot[before + 3], None)
    step(pb, pa, snapshot[before + 2], None)
    step(pa, pb, snapshot[before + 1], None)
    last(pb, snapshot[before], None, 2)


def first_inner(snapshot, guess, sources, velocity, res, base, edge_coef, own_vel, coarse_a, coarse_b, coef, pa, pb):
    t = lax.axis_index("tm")
    inner = (t > 0).astype(F32)
    zero = jnp.zeros((ROWS, LANE), F32)
    for buf in (pa, pb):
        buf[:, :LANE] = zero
        buf[:, PAD - LANE :] = zero
    for n in range(4):
        res[n, :, :LANE] = zero
        res[n, :, PAD - LANE :] = zero
        for c in range(4):
            coef[n, c, :, :LANE] = zero
            coef[n, c, :, PAD - LANE :] = zero
            edge_coef[n, c, :, :LANE] = zero[:16]
            edge_coef[n, c, :, PAD - LANE :] = zero[:16]

    for k in range(4):

        def build(c, carry):
            for r in range(0, ROWS, SUB):
                half = (0.5 * FINE_ADV) * velocity[k, c, r : r + SUB, :].astype(F32)
                for o, value in ((0, FINE_DIFF + half), (1, FINE_DIFF - half)):
                    coef[k, 2 * c + o, r : r + SUB, MID] = value
                    if r == 0:
                        edge_coef[k, 2 * c + o, SUB:, MID] = value
                    if r == ROWS - SUB:
                        edge_coef[k, 2 * c + o, :SUB, MID] = value
            return carry

        lax.fori_loop(0, 2, build, 0)
    at, left, right = chunk_at(t)
    half_lanes = lane_iota(ROWS) < 64
    for k in range(4):
        for c in range(2):
            own_vel[k, c, :, :CHUNK] = velocity[k, c, :, pl.ds(at, CHUNK)]
            x, y = velocity[k, c, :, pl.ds(right, LANE)], velocity[k, c, :, pl.ds(left, LANE)]
            own_vel[k, c, :, CHUNK:] = jnp.where(half_lanes, x.astype(F32), y.astype(F32)).astype(jnp.bfloat16)
    pack_coarse(own_vel, coarse_a, coarse_b)
    width = 1024

    def run(src, snap, use):
        def go(i, carry):
            l0 = i * width
            own = fine_step(src, lambda c, o, w: coef[snap, c, :, pl.ds(o, w)], l0, width)
            use(own, pl.ds(pl.multiple_of(l0, LANE), width), pl.ds(pl.multiple_of(l0 + LANE, LANE), width))
            return carry

        lax.fori_loop(0, COLS // width, go, 0, unroll=True)

    def step(src, dst, snap, source):
        def use(own, at, to):
            if source is not None:
                own = own + sources[source, :, at].astype(F32)
            dst[:, to] = own
            res[3, :, to] = res[3, :, to] + own

        run(src, snap, use)

    def last(src, snap, source, n):
        def use(own, at, to):
            if source is not None:
                own = own + sources[source, :, at].astype(F32)
                base[n, :, at] = own
                own = own - guess[n, :, at]
            res[n, :, to] = own

        run(src, snap, use)

    def start(buf, what):
        if what == "second":
            buf[:, MID] = guess[1]
        elif what == "sources":
            buf[:, MID] = sources[7].astype(F32)
        else:
            buf[:, MID] = guess[0] * inner

    res[3, :, MID] = guess[0] + guess[1] + sources[7].astype(F32)
    relax_chains(t, snapshot, step, last, start, pa, pb)


EDGE = 24


def first_edges(snapshot, guess, sources, in_a, in_b, inner_res, inner_base, edge_coef, pay, base, halo_coef, s_halo, pa, pb, acc, res):
    t = lax.axis_index("tm")
    s = lax.axis_index("space")
    odd = lax.rem(s, 2) == 1
    sub = sub_iota(COLS)
    low = sub < 4
    has_above = (s > 0).astype(F32)
    has_below = (s < lax.axis_size("space") - 1).astype(F32)
    inner = (t > 0).astype(F32)

    def tile(n):
        a = in_a[n * SUB : (n + 1) * SUB, :].astype(F32)
        b = in_b[n * SUB : (n + 1) * SUB, :].astype(F32)
        return jnp.where(odd, b, a), jnp.where(odd, a, b)

    def halves(n):
        below, above = tile(n)
        return jnp.where(low, below, roll4(above)), jnp.where(low, roll4(below), above)

    zero = jnp.zeros((EDGE, LANE), F32)
    for buf in (pa, pb):
        buf[:, :LANE] = zero
        buf[:, PAD - LANE :] = zero
    for k in range(4):
        pair = halves(k)
        for c in range(2):
            for n, value in coefficients(c, pair[c]):
                halo_coef[k, n, :, :LANE] = zero[:SUB]
                halo_coef[k, n, :, PAD - LANE :] = zero[:SUB]
                halo_coef[k, n, :, MID] = value
    g1, g0 = halves(4)
    s_halo[3], s_halo[7] = halves(5)

    def turn(x, by):
        return pltpu.roll(x, by, 0) if by % SUB else x

    for n, k in ((2, 0), (6, 2)):
        (t0, b0), (t1, b1) = tile(k), tile(k + 1)
        value = jnp.where(sub == 0, turn(t0, 1), jnp.where(sub == 1, turn(t1, 2), 0.0))
        s_halo[n] = jnp.where(sub == 6, turn(b0, 2), jnp.where(sub == 7, turn(b1, 3), value))
    below, above = tile(5)
    for n, x, y in ((1, 5, 7), (5, 1, 3)):
        s_halo[n] = jnp.where(sub == 0, turn(below, x), jnp.where(sub == 7, turn(above, y), 0.0))

    width = 1024
    sub_w = sub_iota(width)
    edge = jnp.where(sub_w < 4, has_below, has_above)

    def run(src, snap, use):
        def coef(c, o, w):
            at = pl.ds(o, w)
            return jnp.concatenate(
                [edge_coef[snap, c, :SUB, at], halo_coef[snap, c, :, at], edge_coef[snap, c, SUB:, at]], 0
            )

        def go(i, carry):
            l0 = i * width
            out = fine_step(src, coef, l0, width)
            use(out, pl.ds(pl.multiple_of(l0, LANE), width), pl.ds(pl.multiple_of(l0 + LANE, LANE), width))
            return carry

        lax.fori_loop(0, COLS // width, go, 0, unroll=True)

    def tiles_of(source, at):
        return sources[source, ROWS - SUB :, at].astype(F32), sources[source, :SUB, at].astype(F32)

    def step(src, dst, snap, source):
        def use(out, at, to):
            x, h, y = out[:SUB], out[SUB : 2 * SUB] * edge, out[2 * SUB :]
            if source is not None:
                more = tiles_of(source, at)
                x, y = x + more[0], y + more[1]
                h = h + s_halo[source, :, at]
            dst[:SUB, to] = x
            dst[SUB : 2 * SUB, to] = h
            dst[2 * SUB :, to] = y
            acc[:SUB, at] = acc[:SUB, at] + x
            acc[SUB:, at] = acc[SUB:, at] + y

        run(src, snap, use)

    def last(src, snap, source, n):
        def use(out, at, to):
            x, y = out[:SUB], out[2 * SUB :]
            if source is not None:
                more = tiles_of(source, at)
                x, y = x + more[0], y + more[1]
                lo = sub_w < 4
                base[n, ROWS - SUB :, at] = jnp.where(lo, inner_base[n, ROWS - SUB :, at], x)
                base[n, :SUB, at] = jnp.where(lo, y, inner_base[n, :SUB, at])
                x = x - guess[n, ROWS - SUB :, at]
                y = y - guess[n, :SUB, at]
            res[n, :SUB, to] = x
            res[n, SUB:, to] = y

        run(src, snap, use)

    def start(buf, what):
        if what == "second":
            x, h, y = guess[1, ROWS - SUB :, :], g1, guess[1, :SUB, :]
        elif what == "sources":
            x, y = tiles_of(7, slice(None))
            h = s_halo[7]
        else:
            x, h, y = guess[0, ROWS - SUB :, :] * inner, g0 * inner, guess[0, :SUB, :] * inner
        buf[:SUB, MID] = x
        buf[SUB : 2 * SUB, MID] = h
        buf[2 * SUB :, MID] = y

    x7, y7 = tiles_of(7, slice(None))
    acc[:SUB, :] = guess[0, ROWS - SUB :, :] + guess[1, ROWS - SUB :, :] + x7
    acc[SUB:, :] = guess[0, :SUB, :] + guess[1, :SUB, :] + y7
    for n in range(4):
        res[n, :, :LANE] = zero[:16]
        res[n, :, PAD - LANE :] = zero[:16]
    for n in range(2):
        base[n, SUB : ROWS - SUB, :] = inner_base[n, SUB : ROWS - SUB, :]
    relax_chains(t, snapshot, step, last, start, pa, pb)
    res[3, :, MID] = acc[...]

    lane = lane_iota(SUB)
    lo = sub_iota(LANE) < 4

    def value(n, r, at):
        own = inner_res[n, r : r + SUB, at : at + LANE]
        if r == 0:
            return jnp.where(lo, res[n, SUB:, at : at + LANE], own)
        if r == ROWS - SUB:
            return jnp.where(lo, own, res[n, :SUB, at : at + LANE])
        return own

    for n in range(4):
        for r in range(0, ROWS, SUB):
            for d in range(NDEV):
                at = LANE + d * CHUNK
                for l in range(4):
                    pay[d, pl.ds(piece(n, l) + r, SUB), :] = value(n, r, at + l * LANE)

    def turn(x, by):
        return pltpu.roll(x, by % LANE, 1) if by % LANE else x

    for d in range(NDEV):
        at = LANE + d * CHUNK
        parts = []
        for q in range(12):
            n, r = divmod(q, 4)
            slot = 2 * HALO * (q % 3)
            parts.append(turn(value(n, SUB * r, at + CHUNK), slot))
            parts.append(turn(value(n, SUB * r, at - LANE), slot + 2 * HALO))
        for m in range(4):
            packed = parts[6 * m + 5]
            for k in range(4, -1, -1):
                packed = jnp.where(lane < HALO * (k + 1), parts[6 * m + k], packed)
            pay[d, pl.ds(piece(4, 0) + SUB * m, SUB), :] = packed


HALO = 20
PIECES = 17


def piece(n, l):
    return (4 * n + l) * ROWS


def halo_columns(got, t, n, r):
    m, slot = divmod(4 * n + r // SUB, 3)
    x = got[t, pl.ds(piece(4, 0) + SUB * m, SUB), :]
    right = pltpu.roll(x, LANE - 2 * HALO * slot, 1) if slot else x
    left = pltpu.roll(x, (2 * LANE - 2 * HALO * (slot + 1)) % LANE, 1)
    return jnp.where(lane_iota(SUB) < 64, right, left)


def field_rows(got, t, n, r, count):
    last = jnp.concatenate([halo_columns(got, t, n, r + i) for i in range(0, count, SUB)], 0)
    return jnp.concatenate([*(got[t, pl.ds(piece(n, l) + r, count), :] for l in range(4)), last], 1)


def level_rows(got, j, r):
    t, u = divmod(j, 2)
    value = field_rows(got, t, u, r, SUB)
    if u == 1 and t + 1 < NDEV:
        value = value + field_rows(got, t + 1, 2, r, SUB)
    return value


def pack_residual(got, out_a, out_b):
    odd = lax.rem(lax.axis_index("space"), 2) == 1
    sub = sub_iota(WIDE)
    for n, parts in enumerate(halo_rows()):
        (j, i, a), rest = parts[0], parts[1:]
        top, bottom = level_rows(got, j, SUB * i), level_rows(got, j, 24 - SUB * i)
        for j, i, _ in rest:
            top = jnp.where(sub < a, top, pltpu.roll(level_rows(got, j, SUB * i), a, 0))
            bottom = jnp.where(sub >= SUB - a, bottom, pltpu.roll(level_rows(got, j, 24 - SUB * i), SUB - a, 0))
        out_a[n * SUB : (n + 1) * SUB, :] = jnp.where(odd, top, bottom)
        out_b[n * SUB : (n + 1) * SUB, :] = jnp.where(odd, bottom, top)


def coarse_solve(snapshot, got, velocity, far_a, far_b, got_a, got_b, back, near, vnear, vel, res, mask):
    t = lax.axis_index("tm")
    s = lax.axis_index("space")
    odd = lax.rem(s, 2) == 1
    has_above = (s > 0).astype(F32)
    has_below = (s < lax.axis_size("space") - 1).astype(F32)
    has_left = (t > 0).astype(F32)
    has_right = (t < lax.axis_size("tm") - 1).astype(F32)
    row = lax.broadcasted_iota(jnp.int32, (FAR, WIDE), 0)
    col = lax.broadcasted_iota(jnp.int32, (FAR, WIDE), 1)
    in_rows = jnp.where(row < ROWS, 1.0, jnp.where(row < 52, has_below, has_above))
    in_cols = jnp.where(col < CHUNK, 1.0, jnp.where(col < CHUNK + 64, has_right, has_left))
    mask[...] = in_rows * in_cols

    sub = sub_iota(LANE)
    low = sub < 4

    def tile(n, l):
        at = (slice(n * SUB, (n + 1) * SUB), slice(l * LANE, (l + 1) * LANE))
        a, b = far_a[at].astype(F32), far_b[at].astype(F32)
        return jnp.where(odd, b, a), jnp.where(odd, a, b)

    coarse = 0.5 * COARSE_ADV
    for k in range(4):
        for c in range(2):
            for l in range(5):
                lanes = slice(l * LANE, (l + 1) * LANE)
                own = velocity[k, c, :, lanes].astype(F32)
                q = (k * 2 + c) * 2
                below0, above0 = tile(q, l)
                below1, above1 = tile(q + 1, l)
                edge = jnp.zeros((SUB, LANE), F32)
                if c == 0:
                    below, above = tile(16, l)
                    shifted = pltpu.roll(below, SUB - k, 0) if k else below
                    edge = jnp.where(sub == 0, shifted, edge)
                    edge = jnp.where(sub == 7, pltpu.roll(above, 7 - k, 0), edge)
                vel[k, c, :ROWS, lanes] = coarse * own
                vel[k, c, 32:40, lanes] = coarse * below0
                vel[k, c, 40:48, lanes] = coarse * below1
                vel[k, c, 48:56, lanes] = coarse * edge
                vel[k, c, 56:64, lanes] = coarse * above1
                vel[k, c, 64:72, lanes] = coarse * above0
                vnear[k, c, :ROWS, lanes] = velocity[k, c, :, lanes]
                vnear[k, c, ROWS:, lanes] = jnp.where(low, below0, above0).astype(jnp.bfloat16)

    low_w = sub_iota(WIDE) < 4
    empty = jnp.zeros((SUB, WIDE), F32)
    for j in range(1, NCOARSE):
        if j + 2 <= SUB:
            res[j, 40:48, :] = empty
            res[j, 56:64, :] = empty
        if j + 2 <= 2 * SUB:
            res[j, 48:56, :] = empty
    for n, parts in enumerate(halo_rows()):
        a, b = got_a[n * SUB : (n + 1) * SUB, :], got_b[n * SUB : (n + 1) * SUB, :]
        below, above = jnp.where(odd, b, a), jnp.where(odd, a, b)
        for m, (j, i, _) in enumerate(parts):
            if m:
                used = parts[0][2]
                below, above = pltpu.roll(below, SUB - used, 0), pltpu.roll(above, used, 0)
            if i == 2:
                res[j, 48:56, :] = jnp.where(low_w, below, above)
            else:
                res[j, 32 + SUB * i : 40 + SUB * i, :] = below
                res[j, 64 - SUB * i : 72 - SUB * i, :] = above
    res[0, ROWS:, :] = jnp.zeros((FAR - ROWS, WIDE), F32)
    for j in range(NCOARSE):
        res[j, :ROWS, :] = field_rows(got, j // 2, j % 2, 0, ROWS)

    for l in range(4):
        at = pl.ds(piece(3, l), ROWS)
        total = got[0, at, :]
        for d in range(1, NDEV):
            total = total + got[d, at, :]
        near[0, :ROWS, l * LANE : (l + 1) * LANE] = total

    def send(j, p, e):
        back[j // 2, j % 2] = e[:ROWS, :CHUNK]
        if j:
            near[j, :ROWS, :] = p[:ROWS]
            near[j, ROWS:, :] = jnp.where(low_w, p[32:40], p[p.shape[0] - SUB :])
        near[0, :ROWS, :CHUNK] = near[0, :ROWS, :CHUNK] + p[:ROWS, :CHUNK]

    p = res[NCOARSE - 1]
    send(NCOARSE - 1, p, jnp.zeros_like(p))

    def cut(x):
        return jnp.concatenate([x[:40], x[64:72]], 0)

    for j in range(NCOARSE - 2, -1, -1):
        fit = cut if j <= 5 else lambda x: x
        if j == 5:
            p = cut(p)
        snap = snapshot[4 * j]
        ax, ay = fit(vel.at[snap, 0]), fit(vel.at[snap, 1])
        ax, ay = ax[...], ay[...]
        u = COARSE_DIFF * p
        wx = ax * p
        wy = ay * p
        e = (1.0 - 4.0 * COARSE_DIFF) * p + up(u + wx) + down(u - wx) + east(u + wy) + west(u - wy)
        e = e * fit(mask)[...]
        if j % 2 == 1:
            head = e[:ROWS] + field_rows(got, j // 2 + 1, 2, 0, ROWS)
            e = jnp.concatenate([head, e[ROWS:]], 0)
        p = e + fit(res.at[j])[...]
        send(j, p, e)


def second_relax(snapshot, near, vnear, grad, acc, coef):
    t = lax.axis_index("tm")
    s = lax.axis_index("space")
    has_above = (s > 0).astype(F32)
    has_below = (s < lax.axis_size("space") - 1).astype(F32)
    has_left = (t > 0).astype(F32)
    has_right = (t < lax.axis_size("tm") - 1).astype(F32)
    row = lax.broadcasted_iota(jnp.int32, (NEAR, WIDE), 0)
    col = lax.broadcasted_iota(jnp.int32, (NEAR, WIDE), 1)
    keep = (
        jnp.where(row == 0, has_above, 1.0),
        jnp.where(row == ROWS - 1, has_below, 1.0),
        jnp.where(col == 0, has_left, 1.0),
        jnp.where(col == CHUNK - 1, has_right, 1.0),
    )
    for k in range(4):
        for n in range(4):
            v = (0.5 * FINE_ADV) * vnear[k, n // 2].astype(F32)
            coef[k, n] = keep[n] * (FINE_DIFF - v if n % 2 else FINE_DIFF + v)
    acc[...] = near[0, :ROWS, :CHUNK]

    def interval(j):
        p = near[j + 1]
        total = None
        for k in (3, 2, 1):
            snap = snapshot[4 * j + k]
            c = [coef[snap, n] for n in range(4)]
            p = (1.0 - 4.0 * FINE_DIFF) * p + up(c[0] * p) + down(c[1] * p) + east(c[2] * p) + west(c[3] * p)
            own = p[:ROWS, :CHUNK]
            total = own if total is None else total + own
        return total

    def group(i, carry):
        total = interval(GROUP * i)
        for n in range(1, GROUP):
            total = total + interval(GROUP * i + n)
        acc[...] = acc[...] + total
        return carry

    lax.fori_loop(0, (NCOARSE - 1) // GROUP, group, 0)
    grad[...] = acc[...] * (1.0 / 64.0)


def finish(base, got, out):
    for d in range(NDEV):
        at = slice(d * CHUNK, (d + 1) * CHUNK)
        for u in range(2):
            out[u, :, at] = base[u, :, at] + got[d, u]


def cycle(guess, sources, velocity, snapshot):
    shape = jax.ShapeDtypeStruct
    bf = jnp.bfloat16
    packed = shape((FINE_TILES * SUB, COLS), bf)
    local = [shape(x.shape, x.dtype) for x in (guess, sources, velocity)]
    guess, sources, velocity = (pltpu.with_memory_space_constraint(x, pltpu.MemorySpace.HBM) for x in (guess, sources, velocity))
    fine_a, fine_b, guess, sources, velocity = call(
        pack_fine,
        (packed, packed, *local),
        (guess, sources, velocity),
        (pltpu.SemaphoreType.DMA((13,)),),
        vmem=12,
        space=pltpu.MemorySpace.HBM,
    )
    in_a, in_b = swap(fine_a, fine_b)
    field = lambda rows: pltpu.VMEM((rows, PAD), F32)
    coarse_rows = shape((COARSE_TILES * SUB, WIDE), bf)
    inner_res, inner_base, edge_coef, own_vel, coarse_a, coarse_b = call(
        first_inner,
        (
            shape((4, ROWS, PAD), F32),
            shape((2, ROWS, COLS), F32),
            shape((4, 4, 16, PAD), F32),
            shape((4, 2, ROWS, WIDE), bf),
            coarse_rows,
            coarse_rows,
        ),
        (snapshot, guess, sources, velocity),
        (pltpu.VMEM((4, 4, ROWS, PAD), F32), field(ROWS), field(ROWS)),
        vmem=24,
        flops=200_000_000,
    )
    far_a, far_b = swap(coarse_a, coarse_b)
    pay, base = call(
        first_edges,
        (shape((NDEV, PIECES * ROWS, LANE), F32), shape((2, ROWS, COLS), F32)),
        (snapshot, guess, sources, in_a, in_b, inner_res, inner_base, edge_coef),
        (
            pltpu.VMEM((4, 4, SUB, PAD), F32),
            pltpu.VMEM((8, SUB, COLS), F32),
            field(EDGE),
            field(EDGE),
            pltpu.VMEM((16, COLS), F32),
            pltpu.VMEM((4, 16, PAD), F32),
        ),
        vmem=20,
    )
    got = lax.all_to_all(pay.astype(LINK), "tm", 0, 0, tiled=False).astype(F32)
    tiles = len(halo_rows())
    edges = shape((tiles * SUB, WIDE), F32)
    send_a, send_b = call(pack_residual, (edges, edges), (got,), vmem=12)
    got_a, got_b = swap(send_a.astype(LINK), send_b.astype(LINK))
    back, near, vnear = call(
        coarse_solve,
        (
            shape((NDEV, 2, ROWS, CHUNK), F32),
            shape((NCOARSE, NEAR, WIDE), F32),
            shape((4, 2, NEAR, WIDE), bf),
        ),
        (snapshot, got, own_vel, far_a, far_b, got_a.astype(F32), got_b.astype(F32)),
        (
            pltpu.VMEM((4, 2, FAR, WIDE), F32),
            pltpu.VMEM((NCOARSE, FAR, WIDE), F32),
            pltpu.VMEM((FAR, WIDE), F32),
        ),
        vmem=20,
    )
    returned = lax.all_to_all(back.astype(LINK), "tm", 0, 0, tiled=False)
    grad = call(
        second_relax,
        shape((ROWS, CHUNK), F32),
        (snapshot, near, vnear),
        (pltpu.VMEM((ROWS, CHUNK), F32), pltpu.VMEM((4, 4, NEAR, WIDE), F32)),
        vmem=8,
    )
    c_values = call(finish, shape((2, ROWS, COLS), F32), (base, returned.astype(F32)), vmem=8)
    return c_values, grad


def solution(mesh):
    in_specs = (P("tm", "space", None), P("tm", "space", None), P(None, None, "space", None), P())
    out_specs = (P("tm", "space", None), P("space", "tm"))
    return jax.shard_map(cycle, mesh=mesh, in_specs=in_specs, out_specs=out_specs, check_vma=False)
```
